32 devices in a mesh: gx: 2 (over y), gy: 4 (over x, core), gz: 4 (over z).
Axes of the slice: x: 2, y: 2, z: 4, core: 2. Of those that a mesh axis runs over, the one named last changes fastest.
Arguments:
- velocity: float32 [3, 20, 80, 2560], P(None, 'gx', 'gy', 'gz'), may hold values from -6 to 6
- obstacle_element_mask: int32 [4, 16, 512], P('gx', 'gy', 'gz'), may hold values 0 or 1
- element_metric_scale: float32 [4, 16, 512], P('gx', 'gy', 'gz'), may hold values from 0.5 to 8
Outputs:
- smoothed: float32 [20, 80, 2560], P('gx', 'gy', 'gz')
- coarse: float32 [4, 16, 512], P('gx', 'gy', 'gz')
The draws below stay inside these ranges and needn't reach their ends.
All inputs are finite; a program needn't handle non-finite values. No bound on the sum of `obstacle_element_mask` on one device may be relied on, other than what follows from the above.
Results may differ from the reference program's by a relative error of at most 0.00012.
Values sent between devices are 32-bit elements; how exact they have to be, the bound alone decides.
A program may use at most 384 MiB of HBM per device.

```python
import math
import jax
import jax.numpy as jnp
import numpy as np
from jax import lax

ELEMENTS_X = 4
ELEMENTS_Y = 16
ELEMENTS_Z = 512
NX = 20
NY = 80
NZ = 2560


def plant(values, stream_key, least, top_value):
    shape = values.shape
    spot = [jax.random.randint(jax.random.fold_in(stream_key, axis), (), 0, shape[axis]) for axis in range(len(shape))]
    values = values.at[tuple(spot)].set(least)
    longest = shape.index(max(shape))
    spot[longest] = (spot[longest] + 1) % shape[longest]
    return values.at[tuple(spot)].set(top_value)


def block_levels(own_key, dims, cuts, smallest, largest):
    def one(dim, blocks):
        draws = jax.random.uniform(jax.random.fold_in(jax.random.fold_in(own_key, 6), dim), (blocks,), jnp.float32, smallest / len(cuts), largest / len(cuts))
        return jnp.repeat(jnp.exp(draws), dims[dim] // blocks).reshape((-1,) + (1,) * (len(dims) - dim - 1))

    factor_of = one(*cuts[0])
    for cut in cuts[1:]:
        factor_of = factor_of * one(*cut)
    return factor_of


def bell_draw(key, shape, spread, most, cuts=(), kind=jnp.bfloat16):
    entries = jax.random.normal(key, shape, jnp.float32) * spread
    if len(cuts) > 0:
        entries = block_levels(key, shape, cuts, -0.22, 0.18) * entries
    return jnp.clip(entries, min=-most, max=most).astype(kind)


def setup_inputs(seed: int = 0) -> dict:
    seeds = jax.random.split(jax.random.key(seed), 4)
    velocity = bell_draw(seeds[0], (3, NX, NY, NZ), 1.0, 6.0, ((1, 2), (2, 4), (3, 4)), jnp.float32)
    obstacle_element_mask = plant((jax.random.randint(seeds[1], (ELEMENTS_X, ELEMENTS_Y, ELEMENTS_Z), 0, 8) < 1).astype(jnp.int32), jax.random.fold_in(seeds[1], 1), 0, 1)
    element_metric_scale = jnp.clip(jnp.exp(math.log(8.0) - 2.7725887 * jax.random.uniform(seeds[2], (ELEMENTS_X, ELEMENTS_Y, ELEMENTS_Z), jnp.float32) ** block_levels(seeds[2], (ELEMENTS_X, ELEMENTS_Y, ELEMENTS_Z), ((0, 2), (1, 4), (2, 4)), -0.2, 0.2)), 0.5, 8.0)
    return dict(velocity=velocity, obstacle_element_mask=obstacle_element_mask, element_metric_scale=element_metric_scale)


lift_factor = 10.0
time_step = 0.05
penalty = 4.0

def lobatto_points():
    return np.array([-1.0, -math.sqrt(3.0 / 7.0), 0.0, math.sqrt(3.0 / 7.0), 1.0])

def lobatto_weights():
    return np.array([0.1, 49.0 / 90.0, 32.0 / 45.0, 49.0 / 90.0, 0.1])

def derivative_matrix():
    points = lobatto_points()
    scales = np.array([np.prod([points[i] - points[k] for k in range(5) if k != i]) for i in range(5)])
    result = np.zeros((5, 5))
    for i in range(5):
        for j in range(5):
            if i != j:
                result[i, j] = scales[i] / (scales[j] * (points[i] - points[j]))
        result[i, i] = -np.sum(result[i])
    return result

def eigen_basis_table():
    return np.array([[math.sqrt((1.0 if k == 0 else 2.0) / 5.0) * math.cos(math.pi * (i + 0.5) * k / 5.0) for k in range(5)] for i in range(5)])

def eigen_value_table():
    return np.array([4.0 * math.sin(math.pi * k / 10.0) ** 2 for k in range(5)])

def hat_weight_table():
    points = lobatto_points()
    weights = lobatto_weights()
    return np.array([weights * (1.0 - points) / 2.0, weights * (1.0 + points) / 2.0])

def apply_along(matrix, field, axis):
    weights = jnp.asarray(matrix, jnp.float32)
    out_width = weights.shape[0]
    in_width = weights.shape[1]
    extent = field.shape
    if axis == 0:
        blocks = field.reshape(extent[0] // in_width, in_width, extent[1], extent[2])
        result = jnp.einsum('ij,ajbc->aibc', weights, blocks, precision=lax.Precision.HIGHEST)
        return result.reshape(extent[0] // in_width * out_width, extent[1], extent[2])
    if axis == 1:
        blocks = field.reshape(extent[0], extent[1] // in_width, in_width, extent[2])
        result = jnp.einsum('ij,abjc->abic', weights, blocks, precision=lax.Precision.HIGHEST)
        return result.reshape(extent[0], extent[1] // in_width * out_width, extent[2])
    blocks = field.reshape(extent[0], extent[1], extent[2] // in_width, in_width)
    result = jnp.einsum('ij,abcj->abci', weights, blocks, precision=lax.Precision.HIGHEST)
    return result.reshape(extent[0], extent[1], extent[2] // in_width * out_width)

def to_nodes(values):
    return jnp.repeat(jnp.repeat(jnp.repeat(values, 5, axis=0), 5, axis=1), 5, axis=2)

def face_masks(extent, axis):
    position = jnp.arange(extent) % 5
    layout = [1, 1, 1]
    layout[axis] = extent
    left_end = (position == 0).astype(jnp.float32).reshape(layout)
    right_end = (position == 4).astype(jnp.float32).reshape(layout)
    return (left_end, right_end)

def neighbours(padded, axis):
    inner = padded[1:-1, 1:-1, 1:-1]
    extent = inner.shape[axis]
    lower = [slice(1, -1)] * 3
    upper = [slice(1, -1)] * 3
    lower[axis] = slice(0, extent)
    upper[axis] = slice(2, extent + 2)
    return (inner, padded[tuple(lower)], padded[tuple(upper)])

def convective(padded):
    dmatrix = derivative_matrix()
    terms = []
    for c in range(3):
        total = jnp.zeros(padded.shape[1:], jnp.float32)[1:-1, 1:-1, 1:-1]
        for a in range(3):
            normal_in, normal_lo, normal_hi = neighbours(padded[a], a)
            moved_in, moved_lo, moved_hi = neighbours(padded[c], a)
            flux_in = normal_in * moved_in
            left_end, right_end = face_masks(normal_in.shape[a], a)
            speed_lo = jnp.maximum(jnp.abs(normal_in), jnp.abs(normal_lo))
            speed_hi = jnp.maximum(jnp.abs(normal_in), jnp.abs(normal_hi))
            jump_lo = -0.5 * (normal_lo * moved_lo - flux_in) - 0.5 * speed_lo * (moved_lo - moved_in)
            upper_jump_value = 0.5 * (normal_hi * moved_hi - flux_in) - 0.5 * speed_hi * (moved_hi - moved_in)
            total = total + apply_along(dmatrix, flux_in, a) + lift_factor * (left_end * jump_lo + right_end * upper_jump_value)
        terms.append(total)
    return terms

def divergence(triples):
    dmatrix = derivative_matrix()
    total = 0.0
    for a in range(3):
        inner, lower, upper = triples[a]
        left_end, right_end = face_masks(inner.shape[a], a)
        total = total + apply_along(dmatrix, inner, a) + lift_factor * (left_end * -0.5 * (lower - inner) + right_end * 0.5 * (upper - inner))
    return total

def smooth(pressure_right_side, element_metric_scale):
    basis = eigen_basis_table()
    coeffs = pressure_right_side
    for axis in range(3):
        coeffs = apply_along(basis.T, coeffs, axis)
    extent = pressure_right_side.shape
    modal = jnp.asarray(eigen_value_table(), jnp.float32)
    modes = jnp.tile(modal, extent[0] // 5)[:, None, None] + jnp.tile(modal, extent[1] // 5)[None, :, None] + jnp.tile(modal, extent[2] // 5)[None, None, :]
    coeffs = coeffs / (to_nodes(element_metric_scale) * modes + 1.0)
    for axis in range(3):
        coeffs = apply_along(basis, coeffs, axis)
    return coeffs

def vertex_partials(pressure_right_side):
    hats = hat_weight_table()
    reduced = pressure_right_side
    for axis in range(3):
        reduced = apply_along(hats, reduced, axis)
    extent = reduced.shape
    blocks = reduced.reshape(extent[0] // 2, 2, extent[1] // 2, 2, extent[2] // 2, 2)
    corner_vertex_list = 0.0
    for a in range(2):
        for b in range(2):
            for c in range(2):
                corner_vertex_list = corner_vertex_list + jnp.pad(blocks[:, a, :, b, :, c], ((a, 1 - a), (b, 1 - b), (c, 1 - c)))
    return corner_vertex_list

def reference(velocity, obstacle_element_mask, element_metric_scale):
    padded = jnp.pad(velocity, ((0, 0), (1, 1), (1, 1), (1, 1)))
    damping = 1.0 + penalty * to_nodes(obstacle_element_mask.astype(jnp.float32))
    terms = convective(padded)
    provisional = jnp.stack([(velocity[c] - time_step * terms[c]) / damping for c in range(3)])
    widened = jnp.pad(provisional, ((0, 0), (1, 1), (1, 1), (1, 1)))
    triples = [neighbours(widened[a], a) for a in range(3)]
    pressure_right_side = -divergence(triples)
    smoothed = smooth(pressure_right_side, element_metric_scale)
    corner_vertex_list = vertex_partials(pressure_right_side)
    coarse = corner_vertex_list[:-1, :-1, :-1]
    return (smoothed, coarse)
```

```python
import functools
import itertools
import math

import jax
import jax.numpy as jnp
import numpy as np
from jax import lax
from jax.experimental import pallas as pl
from jax.experimental.pallas import tpu as pltpu
from jax.sharding import PartitionSpec as P

lift_factor = 10.0
time_step = 0.05
penalty = 4.0
half_lift = lift_factor * 0.5
order = 5
names = ("gx", "gy", "gz")
corners = [s for s in itertools.product((0, 1), repeat=3) if any(s)]


def lobatto_points():
    return np.array([-1.0, -math.sqrt(3.0 / 7.0), 0.0, math.sqrt(3.0 / 7.0), 1.0])


def lobatto_weights():
    return np.array([0.1, 49.0 / 90.0, 32.0 / 45.0, 49.0 / 90.0, 0.1])


def derivative_matrix():
    points = lobatto_points()
    scales = np.array(
        [np.prod([points[i] - points[k] for k in range(5) if k != i]) for i in range(5)]
    )
    result = np.zeros((5, 5))
    for i in range(5):
        for j in range(5):
            if i != j:
                result[i, j] = scales[i] / (scales[j] * (points[i] - points[j]))
        result[i, i] = -np.sum(result[i])
    return result


def eigen_basis_table():
    return np.array(
        [
            [
                math.sqrt((1.0 if k == 0 else 2.0) / 5.0) * math.cos(math.pi * (i + 0.5) * k / 5.0)
                for k in range(5)
            ]
            for i in range(5)
        ]
    )


def eigen_value_table():
    return np.array([4.0 * math.sin(math.pi * k / 10.0) ** 2 for k in range(5)])


def hat_weight_table():
    points = lobatto_points()
    weights = lobatto_weights()
    return np.array([weights * (1.0 - points) / 2.0, weights * (1.0 + points) / 2.0])


def mix(coefs, terms):
    total = None
    for coef, term in zip(coefs, terms):
        if abs(coef) < 1e-12:
            continue
        piece = float(coef) * term
        total = piece if total is None else total + piece
    return total


def lifted_derivative(f):
    d = derivative_matrix()
    d[0, 0] += half_lift
    d[4, 4] -= half_lift
    e1, e2 = f[0] + f[4], f[1] + f[3]
    o1, o2 = f[0] - f[4], f[1] - f[3]
    out = [None] * 5
    for i in range(2):
        even = mix(((d[i, 0] + d[i, 4]) / 2, (d[i, 1] + d[i, 3]) / 2, d[i, 2]), (e1, e2, f[2]))
        odd = mix(((d[i, 0] - d[i, 4]) / 2, (d[i, 1] - d[i, 3]) / 2), (o1, o2))
        out[i] = odd + even
        out[4 - i] = odd - even
    out[2] = mix((d[2, 0], d[2, 1]), (o1, o2))
    return out


def to_modes(f):
    s = eigen_basis_table()
    e1, e2 = f[0] + f[4], f[1] + f[3]
    o1, o2 = f[0] - f[4], f[1] - f[3]
    out = []
    for k in range(5):
        if k == 0:
            out.append(float(s[0, 0]) * (e1 + e2 + f[2]))
        elif k % 2 == 0:
            out.append(mix((s[0, k], s[1, k], s[2, k]), (e1, e2, f[2])))
        else:
            out.append(mix((s[0, k], s[1, k]), (o1, o2)))
    return out


def from_modes(c):
    s = eigen_basis_table()
    out = [None] * 5
    base = float(s[0, 0]) * c[0]
    for i in range(2):
        even = base + mix((s[i, 2], s[i, 4]), (c[2], c[4]))
        odd = mix((s[i, 1], s[i, 3]), (c[1], c[3]))
        out[i] = even + odd
        out[4 - i] = even - odd
    out[2] = base + mix((s[2, 2], s[2, 4]), (c[2], c[4]))
    return out


def at_line(a, l, m):
    return ((l, m), (m, l), (m, slice(None), l))[a]


def roll(x, shift, axis):
    size = x.shape[axis]
    shift = shift % size
    return x if shift == 0 else pltpu.roll(x, shift, axis)


class Brick:
    def __init__(self, ex, ey, ez):
        self.ex, self.ey, self.ez = ex, ey, ez
        self.rows = ex * ey

    def iotas(self):
        row = lax.broadcasted_iota(jnp.int32, (self.rows, self.ez), 0)
        lane = lax.broadcasted_iota(jnp.int32, (self.rows, self.ez), 1)
        return row, lane

    def slots(self, a):
        return (self.ex, self.ey, self.ez)[a]

    def packed(self, a, n):
        return -(-n // self.slots(a))

    def step(self, a):
        return (self.ey, 1, 1)[a]

    def place(self, a):
        row, lane = self.iotas()
        return (row // self.ey, row % self.ey, lane)[a]

    def pack(self, face, a, up):
        n = face.shape[0]
        slots, step = self.slots(a), self.step(a)
        axis = 2 if a == 2 else 1
        place = self.place(a)
        start = slots - 1 if up else 0
        groups = []
        if a == 2:
            total = jnp.zeros((self.rows, self.ez), jnp.float32)
            for s in range(n):
                total = jnp.where(place == s, roll(face[s], s - start, 1), total)
            return total[None]
        for g in range(self.packed(a, n)):
            total = None
            for s in range(min(slots, n - g * slots)):
                piece = roll(face[g * slots + s], (s - start) * step, 0)
                total = piece if total is None else jnp.where(place == s, piece, total)
            groups.append(total)
        return jnp.stack(groups)

    def entry(self, packed_ref, n, a, up):
        slots, step = self.slots(a), self.step(a)
        target = 0 if up else slots - 1
        g, s = divmod(n, slots)
        return roll(packed_ref[g], (target - s) * step, 1 if a == 2 else 0)

    def move(self, x, a, up):
        step = self.step(a) if up else -self.step(a)
        return roll(x, step, 1 if a == 2 else 0)

    def edge(self, a, up):
        return self.place(a) == (0 if up else self.slots(a) - 1)


def body(
    brick,
    counts,
    v_ref,
    mask_ref,
    scale_ref,
    pres,
    coarse_ref,
    raw,
    mask_buf,
    scale_buf,
    rows_buf,
    vel,
    conv,
    near,
    far_x,
    raw_x,
    *rest,
):
    send1, recv1, send2, recv2 = rest[0:4], rest[4:8], rest[8:14], rest[14:20]
    send3, recv3 = rest[20], rest[21]
    ssem1, rsem1, ssem2, rsem2, ssem3, rsem3, load_sem, small_sem, ssemx, rsemx = rest[
        22:32
    ]
    ex, ey, ez = brick.ex, brick.ey, brick.ez
    ny = ey * order
    me = [lax.axis_index(name) for name in names]

    def offset_id(shift):
        return tuple(me[a] + shift[a] for a in range(3))

    def exists(shift):
        ok = None
        for a in range(3):
            if shift[a] > 0:
                one = me[a] < counts[a] - 1
            elif shift[a] < 0:
                one = me[a] > 0
            else:
                continue
            ok = one if ok is None else jnp.logical_and(ok, one)
        return ok

    layers = ex * order
    loads = [
        pltpu.make_async_copy(v_ref.at[:, n], raw.at[:, n], load_sem.at[n]) for n in range(layers)
    ]
    small = [
        pltpu.make_async_copy(mask_ref, mask_buf, small_sem.at[0]),
        pltpu.make_async_copy(scale_ref, scale_buf, small_sem.at[1]),
    ]

    unit = [tuple(int(a == b) for b in range(3)) for a in range(3)]
    partners = unit + [tuple(-x for x in u) for u in unit]
    barrier = pltpu.get_barrier_semaphore()
    for shift in partners:

        @pl.when(exists(shift))
        def _():
            pl.semaphore_signal(
                barrier,
                inc=1,
                device_id=offset_id(shift),
                device_id_type=pl.DeviceIdType.MESH,
            )

    for i in range(order):
        for x in range(ex):
            loads[x * order + i].start()
    for copy in small:
        copy.start()

    def transfer(src, dst, ssem, rsem, to):
        copy = pltpu.make_async_remote_copy(
            src_ref=src,
            dst_ref=dst,
            send_sem=ssem,
            recv_sem=rsem,
            device_id=offset_id(to),
            device_id_type=pl.DeviceIdType.MESH,
        )
        return (copy, exists(to), exists(tuple(-x for x in to)), dst)

    def copies(send, recv, ssem, rsem, axes):
        out = []
        for n, a in enumerate(axes):
            for s in range(2):
                d = 2 * n + s
                to = tuple((1 - 2 * s) * u for u in unit[a])
                out.append(transfer(send[d], recv[d], ssem.at[d], rsem.at[d], to))
        return out

    def start(group):
        for copy, has_to, has_source, _ in group:

            @pl.when(has_to)
            def _():
                copy.start()

    def clear(group):
        for _, _, has_source, dst in group:

            @pl.when(jnp.logical_not(has_source))
            def _():
                dst[...] = jnp.zeros_like(dst)

    def arrive(group):
        for copy, has_to, has_source, _ in group:

            @pl.when(has_source)
            def _():
                copy.wait_recv()

    def finish(group):
        for copy, has_to, has_source, _ in group:

            @pl.when(has_to)
            def _():
                copy.wait_send()

    round1x = []
    for c in range(3):
        for s, n in enumerate((layers - 1, 0)):
            to = tuple((1 - 2 * s) * u for u in unit[0])
            d = 2 * c + s
            round1x.append(
                transfer(v_ref.at[c, n], raw_x.at[s, c], ssemx.at[d], rsemx.at[d], to)
            )
    round1 = copies(send1, recv1, ssem1, rsem1, (1, 2))
    round2 = copies(send2, recv2, ssem2, rsem2, (0, 1, 2))
    round3 = [
        transfer(send3.at[n], recv3.at[n], ssem3.at[n], rsem3.at[n], shift)
        for n, shift in enumerate(corners)
    ]

    row, lane = brick.iotas()
    spread = pow(order, -1, ez)
    gather_index = (lane * order) % ez
    scatter_index = (lane * spread) % ez

    def permute(x, index):
        return jnp.take_along_axis(x, index, axis=1, mode="promise_in_bounds")

    tile_of = [(((lane - spread * k) % ez) * order + k) // ez for k in range(order)]

    def split_layer(slab, rows, put, components=(0, 1, 2)):
        for c in components:
            for t in range(order):
                for x in slab:
                    rows[c, t, x * ny : (x + 1) * ny, :] = slab[x](c, slice(t * ez, (t + 1) * ez))
            for j in range(order):
                parts = [
                    permute(rows[c, t, pl.ds(j, brick.rows, stride=order), :], gather_index)
                    for t in range(order)
                ]
                for k in range(order):
                    total = parts[0]
                    for t in range(1, order):
                        total = jnp.where(tile_of[k] == t, parts[t], total)
                    put(c, j, k, roll(total, -spread * k, 1))

    def split(i, carry):
        for x in range(ex):
            n = x * order + i
            pltpu.make_async_copy(v_ref.at[:, n], raw.at[:, n], load_sem.at[n]).wait()

        def reader(x):
            return lambda c, lanes: raw[c, x * order + i, :, lanes]

        def put(c, j, k, value):
            vel[c, i, j, k] = value

        split_layer({x: reader(x) for x in range(ex)}, rows_buf.at[i], put)
        return carry

    lax.fori_loop(0, 2, split, 0)
    pl.semaphore_wait(barrier, sum(exists(shift).astype(jnp.int32) for shift in partners))
    start(round1x)
    lax.fori_loop(2, order, split, 0)

    clear(round1x)
    clear(round1)
    clear(round2)
    clear(round3)
    faces = order * order

    def face_of(ref, a, l):
        index = ((l,), (slice(None), l), (slice(None), slice(None), l))[a]
        return ref[index]

    for a in (2, 1):
        for s in range(2):
            l = order - 1 if s == 0 else 0
            face = jnp.concatenate(
                [face_of(vel.at[c], a, l).reshape(faces, brick.rows, ez) for c in range(3)]
            )
            send1[2 * (a - 1) + s][...] = brick.pack(face, a, s == 0)
        start(round1[2 * (a - 1) : 2 * a])

    def inner_axis(a):
        def run(m, carry):
            normal = [vel[(a,) + at_line(a, l, m)] for l in range(order)]
            for c in range(3):
                if c == a:
                    flux = [x * x for x in normal]
                else:
                    flux = [normal[l] * vel[(c,) + at_line(a, l, m)] for l in range(order)]
                out = lifted_derivative(flux)
                for l in range(order):
                    where = (c,) + at_line(a, l, m)
                    conv[where] = out[l] if a == 0 else conv[where] + out[l]
            return carry

        lax.fori_loop(0, order, run, 0)

    for a in range(3):
        inner_axis(a)

    for copy in small:
        copy.wait()
    solid = jnp.concatenate([mask_buf[x] for x in range(ex)], axis=0).astype(jnp.float32)
    scale = jnp.concatenate([scale_buf[x] for x in range(ex)], axis=0)
    fluid = 1.0 / (1.0 + penalty * solid)

    def face_terms(a, components=(0, 1, 2)):
        for s in range(2):
            up = s == 0
            edge = brick.edge(a, up)
            own, other = (0, order - 1) if up else (order - 1, 0)
            for c in components:
                for m in range(order):
                    line = vel[(c,) + at_line(a, other, m)]
                    for q in range(order):
                        n = (c * order + m) * order + q
                        if a == 0:
                            far = far_x[c, m, q]
                        else:
                            far = brick.entry(recv1[2 * (a - 1) + s], n, a, up)
                        near[s, c, m, q] = jnp.where(edge, far, brick.move(line[q], a, up))

            def add_faces(m, carry):
                normal = vel[(a,) + at_line(a, own, m)]
                normal_out = near[s, a, m]
                speed = jnp.maximum(jnp.abs(normal), jnp.abs(normal_out))
                for c in components:
                    moved = vel[(c,) + at_line(a, own, m)]
                    moved_out = near[s, c, m]
                    jump = speed * (moved_out - moved)
                    flux = normal_out * moved_out
                    where = (c,) + at_line(a, own, m)
                    if up:
                        conv[where] = conv[where] - half_lift * (flux + jump)
                    else:
                        conv[where] = conv[where] + half_lift * (flux - jump)
                return carry

            lax.fori_loop(0, order, add_faces, 0, unroll=True)

    def advance(c, i):
        conv[c, i] = (vel[c, i] - time_step * conv[c, i]) * fluid

    for a in (2, 1):
        arrive(round1[2 * (a - 1) : 2 * a])
        face_terms(a)
    for c in range(3):
        for i in range(1, order - 1):
            advance(c, i)

    def reader_x(side):
        return lambda c, lanes: raw_x[side, c, :, lanes]

    def put_x(c, j, k, value):
        far_x[c, j, k] = value

    for a in range(3):
        arrive(round1x[2 * a : 2 * a + 2])
        split_layer({0: reader_x(0), ex - 1: reader_x(1)}, rows_buf.at[0], put_x, (a,))
        face_terms(0, (a,))
        advance(a, 0)
        advance(a, order - 1)
        for s in range(2):
            l = order - 1 if s == 0 else 0
            face = face_of(conv.at[a], a, l).reshape(faces, brick.rows, ez)
            send2[2 * a + s][...] = brick.pack(face, a, s == 0)
        start(round2[2 * a : 2 * a + 2])

    for a in range(3):

        def diverge(m, carry):
            out = lifted_derivative([conv[(a,) + at_line(a, l, m)] for l in range(order)])
            for l in range(order):
                where = at_line(a, l, m)
                pres[where] = -out[l] if a == 0 else pres[where] - out[l]
            return carry

        lax.fori_loop(0, order, diverge, 0, unroll=True)

    for a in range(3):
        arrive(round2[2 * a : 2 * a + 2])
        for s in range(2):
            up = s == 0
            edge = brick.edge(a, up)
            own, other = (0, order - 1) if up else (order - 1, 0)
            for m in range(order):
                line = conv[(a,) + at_line(a, other, m)]
                values = []
                for q in range(order):
                    far = brick.entry(recv2[2 * a + s], m * order + q, a, up)
                    values.append(jnp.where(edge, far, brick.move(line[q], a, up)))
                side = jnp.stack(values)
                where = at_line(a, own, m)
                if up:
                    pres[where] = pres[where] + half_lift * side
                else:
                    pres[where] = pres[where] - half_lift * side

    hats = hat_weight_table()
    by_x = []
    for i in range(order):
        slab = [pres[i, j] for j in range(order)]
        along_y = [mix(hats[b], slab) for b in range(2)]
        by_x.append([[mix(hats[c], [along_y[b][k] for k in range(order)]) for c in range(2)] for b in range(2)])
    parts = {
        (a, b, c): mix(hats[a], [by_x[i][b][c] for i in range(order)])
        for a in range(2)
        for b in range(2)
        for c in range(2)
    }
    for a in (2, 1, 0):
        edge = brick.edge(a, True)
        merged = {}
        for key in parts:
            if key[a] == 1:
                continue
            upper = key[:a] + (1,) + key[a + 1 :]
            moved = brick.move(parts[upper], a, True)
            if a == 1:
                swap = roll(parts[upper], 1 - ey, 0)
                moved = jnp.where(edge, swap, moved)
            merged[key] = parts[key] + jnp.where(edge, 0.0, moved)
            merged[upper] = jnp.where(edge, moved, 0.0)
        parts = merged
    for n, shift in enumerate(corners):
        send3[n] = parts[shift]
    start(round3)

    basis_values = eigen_value_table()

    def forward(i, carry):
        slab = to_modes([pres[i, j] for j in range(order)])
        for j in range(order):
            out = to_modes([slab[j][k] for k in range(order)])
            for k in range(order):
                pres[i, j, k] = out[k]
        return carry

    lax.fori_loop(0, order, forward, 0)

    for j in range(order):
        modes = to_modes([pres[i, j] for i in range(order)])
        scaled = []
        for i in range(order):
            denominator = jnp.stack(
                [
                    scale * float(basis_values[i] + basis_values[j] + basis_values[k]) + 1.0
                    for k in range(order)
                ]
            )
            scaled.append(modes[i] / denominator)
        out = from_modes(scaled)
        for i in range(order):
            pres[i, j] = out[i]

    arrive(round3)
    total = parts[(0, 0, 0)]
    for n in range(len(corners)):
        total = total + recv3[n]
    for x in range(ex):
        coarse_ref[x] = total[x * ey : (x + 1) * ey]
    finish(round1x)
    finish(round1)
    finish(round2)
    finish(round3)


def finish_body(brick, pres, coarse_in, smooth_ref, coarse_ref, rows_buf):
    ex, ey, ez = brick.ex, brick.ey, brick.ez
    ny = ey * order
    row, lane = brick.iotas()
    spread = pow(order, -1, ez)
    scatter_index = (lane * spread) % ez
    tile_of = [(((lane - spread * k) % ez) * order + k) // ez for k in range(order)]

    def permute(x, index):
        return jnp.take_along_axis(x, index, axis=1, mode="promise_in_bounds")

    coarse_ref[...] = coarse_in[...]

    def backward(i, carry):
        slab = from_modes([pres[i, j] for j in range(order)])
        for j in range(order):
            out = from_modes([slab[j][k] for k in range(order)])
            rolled = [roll(out[k], spread * k, 1) for k in range(order)]
            for t in range(order):
                total = rolled[0]
                for k in range(1, order):
                    total = jnp.where(tile_of[k] == t, rolled[k], total)
                rows_buf[i, t, pl.ds(j, brick.rows, stride=order), :] = permute(
                    total, scatter_index
                )
        for t in range(order):
            for x in range(ex):
                smooth_ref[x * order + i, :, t * ez : (t + 1) * ez] = rows_buf[
                    i, t, x * ny : (x + 1) * ny, :
                ]
        return carry

    lax.fori_loop(0, order, backward, 0)


def shards(counts, velocity, mask, scale):
    ex, ey, ez = mask.shape
    brick = Brick(ex, ey, ez)
    tile = (brick.rows, ez)
    faces = order * order

    def buffers(n):
        return [
            pltpu.VMEM((brick.packed(a, n),) + tile, jnp.float32)
            for a in range(3)
            for _ in range(2)
        ]

    whole = pl.BlockSpec(memory_space=pltpu.VMEM)
    remote = pl.BlockSpec(memory_space=pltpu.HBM)
    sems = pltpu.SemaphoreType.DMA
    f32 = jnp.float32
    layer = velocity.shape[2:]
    modes, coarse = pl.pallas_call(
        functools.partial(body, brick, counts),
        out_shape=(
            jax.ShapeDtypeStruct((order, order, order) + tile, f32),
            jax.ShapeDtypeStruct(mask.shape, f32),
        ),
        in_specs=[remote] * 3,
        out_specs=(whole, whole),
        scratch_shapes=[
            pltpu.VMEM(velocity.shape, f32),
            pltpu.VMEM(mask.shape, jnp.int32),
            pltpu.VMEM(scale.shape, f32),
            pltpu.VMEM((order, 3, order, brick.rows * order, ez), f32),
            pltpu.VMEM((3, order, order, order) + tile, f32),
            pltpu.VMEM((3, order, order, order) + tile, f32),
            pltpu.VMEM((2, 3, order, order) + tile, f32),
            pltpu.VMEM((3, order, order) + tile, f32),
            pltpu.VMEM((2, 3) + layer, f32),
        ]
        + buffers(3 * faces)[2:]
        + buffers(3 * faces)[2:]
        + buffers(faces)
        + buffers(faces)
        + [pltpu.VMEM((len(corners),) + tile, f32)] * 2
        + [sems((6,))] * 4
        + [sems((len(corners),))] * 2
        + [sems((ex * order,)), sems((2,)), sems((6,)), sems((6,))],
        compiler_params=pltpu.CompilerParams(
            collective_id=0, has_side_effects=True, vmem_limit_bytes=24 << 20
        ),
    )(*[pltpu.with_memory_space_constraint(z, pltpu.HBM) for z in (velocity, mask, scale)])

    return pl.pallas_call(
        functools.partial(finish_body, brick),
        out_shape=(
            jax.ShapeDtypeStruct(velocity.shape[1:], f32),
            jax.ShapeDtypeStruct(mask.shape, f32),
        ),
        in_specs=[whole] * 2,
        out_specs=(whole, whole),
        scratch_shapes=[pltpu.VMEM((order, order, brick.rows * order, ez), f32)],
        compiler_params=pltpu.CompilerParams(vmem_limit_bytes=16 << 20),
    )(modes, coarse)


def solution(mesh):
    counts = tuple(mesh.shape[name] for name in names)
    return jax.shard_map(
        functools.partial(shards, counts),
        mesh=mesh,
        in_specs=(P(None, "gx", "gy", "gz"), P("gx", "gy", "gz"), P("gx", "gy", "gz")),
        out_specs=(P("gx", "gy", "gz"), P("gx", "gy", "gz")),
        check_vma=False,
    )
```

```python
import functools
import itertools
import math

import jax
import jax.numpy as jnp
import numpy as np
from jax import lax
from jax.experimental import pallas as pl
from jax.experimental.pallas import tpu as pltpu
from jax.sharding import PartitionSpec as P

lift_factor = 10.0
time_step = 0.05
penalty = 4.0
half_lift = lift_factor * 0.5
order = 5
names = ("gx", "gy", "gz")
corners = [s for s in itertools.product((0, 1), repeat=3) if any(s)]
x_order = (0, 2, 1)


def lobatto_points():
    return np.array([-1.0, -math.sqrt(3.0 / 7.0), 0.0, math.sqrt(3.0 / 7.0), 1.0])


def lobatto_weights():
    return np.array([0.1, 49.0 / 90.0, 32.0 / 45.0, 49.0 / 90.0, 0.1])


def derivative_matrix():
    points = lobatto_points()
    scales = np.array(
        [np.prod([points[i] - points[k] for k in range(5) if k != i]) for i in range(5)]
    )
    result = np.zeros((5, 5))
    for i in range(5):
        for j in range(5):
            if i != j:
                result[i, j] = scales[i] / (scales[j] * (points[i] - points[j]))
        result[i, i] = -np.sum(result[i])
    return result


def eigen_value_table():
    return np.array([4.0 * math.sin(math.pi * k / 10.0) ** 2 for k in range(5)])


def hat_weight_table():
    points = lobatto_points()
    weights = lobatto_weights()
    return np.array([weights * (1.0 - points) / 2.0, weights * (1.0 + points) / 2.0])


def mix(coefs, terms):
    total = None
    for coef, term in zip(coefs, terms):
        if abs(coef) < 1e-12:
            continue
        piece = float(coef) * term
        total = piece if total is None else total + piece
    return total


def lifted_derivative(f, factor):
    d = derivative_matrix()
    d[0, 0] += half_lift
    d[4, 4] -= half_lift
    d = d * factor
    e1, e2 = f[0] + f[4], f[1] + f[3]
    o1, o2 = f[0] - f[4], f[1] - f[3]
    out = [None] * 5
    for i in range(2):
        even = mix(((d[i, 0] + d[i, 4]) / 2, (d[i, 1] + d[i, 3]) / 2, d[i, 2]), (e1, e2, f[2]))
        odd = mix(((d[i, 0] - d[i, 4]) / 2, (d[i, 1] - d[i, 3]) / 2), (o1, o2))
        out[i] = odd + even
        out[4 - i] = odd - even
    out[2] = mix((d[2, 0], d[2, 1]), (o1, o2))
    return out


cos18, cos54 = math.cos(math.pi * 0.1), math.cos(math.pi * 0.3)
cos36, cos72 = math.cos(math.pi * 0.2), math.cos(math.pi * 0.4)
even_gain = (cos36 + cos72) / 2
odd_ratio = cos54 / cos18
norm_squares = [0.2, 0.4 * cos18**2, 0.4, 0.4 * cos18**2, 0.4]


def to_modes(f):
    e1, e2 = f[0] + f[4], f[1] + f[3]
    o1, o2 = f[0] - f[4], f[1] - f[3]
    s = e1 + e2
    p = even_gain * (e1 - e2)
    q = 0.25 * s - f[2]
    return [s + f[2], o1 + odd_ratio * o2, p + q, odd_ratio * o1 - o2, p - q]


def from_modes(c):
    s, d = c[2] + c[4], c[2] - c[4]
    p = even_gain * s
    base = c[0] + 0.25 * d
    even = (base + p, base - p)
    odd = (c[1] + odd_ratio * c[3], odd_ratio * c[1] - c[3])
    return [even[0] + odd[0], even[1] + odd[1], c[0] - d, even[1] - odd[1], even[0] - odd[0]]


def at_line(a, l, m):
    return ((l, m), (m, l), (m, slice(None), l))[a]


def roll(x, shift, axis):
    size = x.shape[axis]
    shift = shift % size
    return x if shift == 0 else pltpu.roll(x, shift, axis)


class Brick:
    def __init__(self, ex, ey, ez):
        self.ex, self.ey, self.ez = ex, ey, ez
        self.rows = ex * ey
        self.ny = ey * order
        self.pitch = -(-self.ny // 8) * 8

    def iotas(self):
        row = lax.broadcasted_iota(jnp.int32, (self.rows, self.ez), 0)
        lane = lax.broadcasted_iota(jnp.int32, (self.rows, self.ez), 1)
        return row, lane

    def slots(self, a):
        return (self.ex, self.ey, self.ez)[a]

    def place(self, a):
        row, lane = self.iotas()
        return (row // self.ey, row % self.ey, lane)[a]

    def move(self, x, a, up):
        step = (self.ey, 1, 1)[a]
        return roll(x, step if up else -step, x.ndim - (1 if a == 2 else 2))

    def edge(self, a, up):
        return self.place(a) == (0 if up else self.slots(a) - 1)


def body(
    brick,
    counts,
    v_ref,
    mask_ref,
    scale_ref,
    out_ref,
    coarse_ref,
    raw,
    mask_buf,
    scale_buf,
    vel,
    conv,
    far_x,
    far_y,
    send_z,
    far_z,
    shifted,
    gain,
    pres,
    inverse,
    far2_x,
    far2_y,
    send2_z,
    far2_z,
    send3,
    recv3,
    *sems,
):
    (load_sem, small_sem, sx, rx, sy, ry, sz, rz, s2x, r2x, s2y, r2y, s2z, r2z, s3, r3) = sems
    ex, ey, ez, rows, ny, pitch = brick.ex, brick.ey, brick.ez, brick.rows, brick.ny, brick.pitch
    me = [lax.axis_index(name) for name in names]

    def exists(shift):
        ok = None
        for a in range(3):
            if shift[a] > 0:
                one = me[a] < counts[a] - 1
            elif shift[a] < 0:
                one = me[a] > 0
            else:
                continue
            ok = one if ok is None else jnp.logical_and(ok, one)
        return ok

    def device(shift):
        return tuple(me[a] + shift[a] for a in range(3))

    unit = [tuple(int(a == b) for b in range(3)) for a in range(3)]

    def toward(a, s):
        return tuple((1 - 2 * s) * u for u in unit[a])

    partners = [toward(a, s) for a in range(3) for s in range(2)]
    barrier = pltpu.get_barrier_semaphore()
    for shift in partners:

        @pl.when(exists(shift))
        def _():
            pl.semaphore_signal(
                barrier, inc=1, device_id=device(shift), device_id_type=pl.DeviceIdType.MESH
            )

    loads = {}
    for c in x_order:
        for x in range(ex):
            for t in range(order):
                loads[c, x, t] = pltpu.make_async_copy(
                    v_ref.at[c, x * order : (x + 1) * order, :, t * ez : (t + 1) * ez],
                    raw.at[c, :, t, x * pitch : x * pitch + ny],
                    load_sem.at[(c * ex + x) * order + t],
                )
                loads[c, x, t].start()
    small = [
        pltpu.make_async_copy(mask_ref, mask_buf, small_sem.at[0]),
        pltpu.make_async_copy(scale_ref, scale_buf, small_sem.at[1]),
    ]
    for copy in small:
        copy.start()

    class Group:
        def __init__(self, shift, triples, dst):
            self.to, self.source = exists(shift), exists(tuple(-x for x in shift))
            self.dst = dst
            self.copies = [
                pltpu.make_async_remote_copy(
                    src_ref=src,
                    dst_ref=to,
                    send_sem=ssem,
                    recv_sem=rsem,
                    device_id=device(shift),
                    device_id_type=pl.DeviceIdType.MESH,
                )
                for src, to, ssem, rsem in triples
            ]

        def start(self):
            @pl.when(self.to)
            def _():
                for copy in self.copies:
                    copy.start()

        def clear(self):
            @pl.when(jnp.logical_not(self.source))
            def _():
                self.dst[...] = jnp.zeros_like(self.dst)

        def arrive(self):
            @pl.when(self.source)
            def _():
                for copy in self.copies:
                    copy.wait_recv()

        def finish(self):
            @pl.when(self.to)
            def _():
                for copy in self.copies:
                    copy.wait_send()

    def x_rows(s):
        top = (ex - 1) * ey
        return [(top + e, e) if s == 0 else (e, top + e) for e in range(ey)]

    def y_rows(s):
        return [
            (x * ey + ey - 1, x * ey) if s == 0 else (x * ey, x * ey + ey - 1) for x in range(ex)
        ]

    def face(s):
        return order - 1 if s == 0 else 0

    round1x, round1, round2, round3 = {}, {}, {}, {}
    for s in range(2):
        for c in range(3):
            n = (c * 2 + s) * ey
            round1x[c, s] = Group(
                toward(0, s),
                [
                    (
                        vel.at[c, face(s), :, :, src],
                        far_x.at[s, c, :, :, dst],
                        sx.at[n + e],
                        rx.at[n + e],
                    )
                    for e, (src, dst) in enumerate(x_rows(s))
                ],
                far_x.at[s, c],
            )
        round1[1, s] = Group(
            toward(1, s),
            [
                (
                    vel.at[:, :, face(s), :, src],
                    far_y.at[s, :, :, :, dst],
                    sy.at[s * ex + x],
                    ry.at[s * ex + x],
                )
                for x, (src, dst) in enumerate(y_rows(s))
            ],
            far_y.at[s],
        )
        round1[2, s] = Group(
            toward(2, s), [(send_z.at[s], far_z.at[s], sz.at[s], rz.at[s])], far_z.at[s]
        )
        round2[0, s] = Group(
            toward(0, s),
            [
                (
                    conv.at[0, face(s), :, :, src],
                    far2_x.at[s, :, :, dst],
                    s2x.at[s * ey + e],
                    r2x.at[s * ey + e],
                )
                for e, (src, dst) in enumerate(x_rows(s))
            ],
            far2_x.at[s],
        )
        round2[1, s] = Group(
            toward(1, s),
            [
                (
                    conv.at[1, :, face(s), :, src],
                    far2_y.at[s, :, :, dst],
                    s2y.at[s * ex + x],
                    r2y.at[s * ex + x],
                )
                for x, (src, dst) in enumerate(y_rows(s))
            ],
            far2_y.at[s],
        )
        round2[2, s] = Group(
            toward(2, s), [(send2_z.at[s], far2_z.at[s], s2z.at[s], r2z.at[s])], far2_z.at[s]
        )
    for n, shift in enumerate(corners):
        round3[n] = Group(
            shift, [(send3.at[n], recv3.at[n], s3.at[n], r3.at[n])], recv3.at[n]
        )

    def each(groups, act):
        for key in groups:
            getattr(groups[key], act)()

    def pick(groups, a):
        return {key: groups[key] for key in groups if key[0] == a}

    row, lane = brick.iotas()
    spread = pow(order, -1, ez)
    turn = pow(ez, -1, order)
    phase = (turn * lane) % order
    bits = [(phase & bit) != 0 for bit in (1, 2, 4)]
    place_x = brick.place(0)

    def permute(x, index):
        return jnp.take_along_axis(x, index, axis=1, mode="promise_in_bounds")

    def barrel(tiles, sign):
        for bit, on in zip((1, 2, 4), bits):
            tiles = [jnp.where(on, tiles[(m - sign * bit) % order], tiles[m]) for m in range(order)]
        return tiles

    def pack_entry(total, tile, n, s):
        start = ez - 1 if s == 0 else 0
        return jnp.where(lane == n, roll(tile, n - start, 1), total)

    def unpack_entry(packed, n, s):
        return roll(packed, (0 if s == 0 else ez - 1) - n, 1)

    zero = jnp.zeros((rows, ez), jnp.float32)

    packs = [zero, zero]
    for c in x_order:
        for x in range(ex):
            for t in range(order):
                loads[c, x, t].wait()
        for i in (4, 0, 1, 2, 3):
            merged = []
            for j in range(order):
                natural = []
                for t in range(order):
                    tile = None
                    for x in range(ex):
                        start = j + x * (pitch - ny)
                        part = raw[c, i, t, pl.ds(start, rows, stride=order), :]
                        tile = part if x == 0 else jnp.where(place_x == x, part, tile)
                    natural.append(tile)
                merged.append(barrel(natural, 1))
            for k in range(order):
                index = (lane * order + k) % ez
                for j in range(order):
                    tile = permute(merged[j][(turn * k) % order], index)
                    vel[c, i, j, k] = tile
                    n = (c * order + i) * order + j
                    for s in range(2):
                        if k == face(s):
                            packs[s] = pack_entry(packs[s], tile, n, s)
    for s in range(2):
        send_z[s] = packs[s]

    pl.semaphore_wait(barrier, sum(exists(shift).astype(jnp.int32) for shift in partners))
    each(pick(round1x, x_order[0]), "start")
    each(round1, "start")
    for c in x_order[1:]:
        each(pick(round1x, c), "start")

    each(round1x, "clear")
    each(round1, "clear")
    each(round2, "clear")
    each(round3, "clear")

    def inner_axis(a):
        def run(m, carry):
            normal = [vel[(a,) + at_line(a, l, m)] for l in range(order)]
            for c in range(3):
                if c == a:
                    moved = normal
                else:
                    moved = [vel[(c,) + at_line(a, l, m)] for l in range(order)]
                out = lifted_derivative([n * w for n, w in zip(normal, moved)], -time_step)
                for l in range(order):
                    where = (c,) + at_line(a, l, m)
                    conv[where] = (moved[l] if a == 0 else conv[where]) + out[l]
                if a == 2:
                    for s in range(2):
                        shifted[s, c, m] = brick.move(moved[face(s)], 2, s == 0)
            return carry

        lax.fori_loop(0, order, run, 0)

    for a in range(3):
        inner_axis(a)

    for copy in small:
        copy.wait()
    solid = jnp.concatenate([mask_buf[x] for x in range(ex)], axis=0).astype(jnp.float32)
    scale = jnp.concatenate([scale_buf[x] for x in range(ex)], axis=0)
    fluid = 1.0 / (1.0 + penalty * solid)

    eigen = eigen_value_table()
    slot_of = {}
    for key in itertools.combinations_with_replacement(range(order), 3):
        slot_of[key] = len(slot_of)
        size = float(np.prod([norm_squares[k] for k in key]))
        inverse[slot_of[key]] = 1.0 / (scale * float(sum(eigen[k] for k in key) / size) + 1.0 / size)

    edges = [[brick.edge(a, s == 0) for s in range(2)] for a in range(3)]

    def near(a, s, c, m):
        other = face(s)
        if a == 2:
            tiles = [
                jnp.where(
                    edges[2][s],
                    unpack_entry(far_z[s], (c * order + m) * order + q, s),
                    shifted[s, c, m, q],
                )
                for q in range(order)
            ]
            return jnp.stack(tiles)
        far = far_x[s, c, m] if a == 0 else far_y[s, c, m]
        return jnp.where(edges[a][s], far, brick.move(vel[(c,) + at_line(a, other, m)], a, s == 0))

    step_lift = time_step * half_lift

    def face_terms(a, components):
        for s in range(2):
            own = order - 1 - face(s)
            for m in range(order):
                outside = None
                if a > 0 or components[0] == 0:
                    normal = vel[(a,) + at_line(a, own, m)]
                    outside = near(a, s, a, m)
                    down = step_lift * jnp.maximum(jnp.abs(normal), jnp.abs(outside))
                    flow = step_lift * outside
                    across = down + flow if s == 0 else down - flow
                    if a == 0:
                        gain[s, 0, m] = across
                        gain[s, 1, m] = down
                else:
                    across, down = gain[s, 0, m], gain[s, 1, m]
                for c in components:
                    moved_out = outside if c == a else near(a, s, c, m)
                    where = (c,) + at_line(a, own, m)
                    conv[where] = conv[where] + (across * moved_out - down * vel[where])

    def advance(c, i):
        conv[c, i] = conv[c, i] * fluid

    for a in (1, 2):
        each(pick(round1, a), "arrive")
        face_terms(a, (0, 1, 2))
    for c in range(3):
        for i in range(1, order - 1):
            advance(c, i)

    def diverge(a, lines):
        for m in lines:
            out = lifted_derivative([conv[(a,) + at_line(a, l, m)] for l in range(order)], -1.0)
            for l in range(order):
                where = at_line(a, l, m)
                pres[where] = out[l] if a == 0 else pres[where] + out[l]

    packs2 = [zero, zero]

    def pack2(i, packs2):
        for j in range(order):
            for s in range(2):
                packs2[s] = pack_entry(packs2[s], conv[2, i, j, face(s)], i * order + j, s)

    for c in x_order:
        each(pick(round1x, c), "arrive")
        face_terms(0, (c,))
        advance(c, 0)
        advance(c, order - 1)
        if c == 2:
            pack2(0, packs2)
            pack2(order - 1, packs2)
            for s in range(2):
                send2_z[s] = packs2[s]
        each(pick(round2, c), "start")
        if c == 0:
            diverge(0, range(order))
            for i in range(1, order - 1):
                pack2(i, packs2)
            diverge(1, range(1, order - 1))
            diverge(2, range(1, order - 1))
        else:
            diverge(c, (0, order - 1))

    for a in (0, 2, 1):
        each(pick(round2, a), "arrive")
        for s in range(2):
            own = order - 1 - face(s)
            for m in range(order):
                line = conv[(a,) + at_line(a, face(s), m)]
                if a == 2:
                    far = jnp.stack(
                        [unpack_entry(far2_z[s], m * order + q, s) for q in range(order)]
                    )
                else:
                    far = far2_x[s, m] if a == 0 else far2_y[s, m]
                side = jnp.where(edges[a][s], far, brick.move(line, a, s == 0))
                where = at_line(a, own, m)
                if s == 0:
                    pres[where] = pres[where] + half_lift * side
                else:
                    pres[where] = pres[where] - half_lift * side

    hats = hat_weight_table()
    by_x = []
    for i in range(order):
        slab = [pres[i, j] for j in range(order)]
        along_y = [mix(hats[b], slab) for b in range(2)]
        by_x.append(
            [
                [mix(hats[c], [along_y[b][k] for k in range(order)]) for c in range(2)]
                for b in range(2)
            ]
        )
    parts = {
        (a, b, c): mix(hats[a], [by_x[i][b][c] for i in range(order)])
        for a in range(2)
        for b in range(2)
        for c in range(2)
    }
    for a in (2, 1, 0):
        edge = edges[a][0]
        merged = {}
        for key in parts:
            if key[a] == 1:
                continue
            upper = key[:a] + (1,) + key[a + 1 :]
            moved = brick.move(parts[upper], a, True)
            if a == 1:
                moved = jnp.where(edge, roll(parts[upper], 1 - ey, 0), moved)
            merged[key] = parts[key] + jnp.where(edge, 0.0, moved)
            merged[upper] = jnp.where(edge, moved, 0.0)
        parts = merged
    for n, shift in enumerate(corners):
        send3[n] = parts[shift]
    each(round3, "start")

    def forward(i, carry):
        slab = to_modes([pres[i, j] for j in range(order)])
        for j in range(order):
            out = to_modes([slab[j][k] for k in range(order)])
            for k in range(order):
                pres[i, j, k] = out[k]
        return carry

    lax.fori_loop(0, order, forward, 0)

    for j in range(order):
        for k in range(order):
            modes = to_modes([pres[i, j, k] for i in range(order)])
            modes = [
                modes[i] * inverse[slot_of[tuple(sorted((i, j, k)))]] for i in range(order)
            ]
            out = from_modes(modes)
            for i in range(order):
                pres[i, j, k] = out[i]

    for i in range(order):
        slab = from_modes([pres[i, j] for j in range(order)])
        lines = [from_modes([slab[j][k] for k in range(order)]) for j in range(order)]
        mixed = [[None] * order for _ in range(order)]
        for k in range(order):
            index = ((lane + (ez - k)) * spread) % ez
            for j in range(order):
                mixed[j][(turn * k) % order] = permute(lines[j][k], index)
        for j in range(order):
            natural = barrel(mixed[j], -1)
            for t in range(order):
                for x in range(ex):
                    out_ref[i, t, pl.ds(x * pitch + j, ey, stride=order), :] = natural[t][
                        x * ey : (x + 1) * ey
                    ]

    each(round3, "arrive")
    total = parts[(0, 0, 0)]
    for n in range(len(corners)):
        total = total + recv3[n]
    for x in range(ex):
        coarse_ref[x] = total[x * ey : (x + 1) * ey]
    each(round1x, "finish")
    each(round1, "finish")
    each(round2, "finish")
    each(round3, "finish")


def deliver(brick, packed_ref, part_ref, smooth_ref, coarse_ref, sems):
    ez, ny, pitch = brick.ez, brick.ny, brick.pitch
    copies = [pltpu.make_async_copy(part_ref, coarse_ref, sems.at[0])]
    for x in range(brick.ex):
        for t in range(order):
            copies.append(
                pltpu.make_async_copy(
                    packed_ref.at[:, t, x * pitch : x * pitch + ny],
                    smooth_ref.at[x * order : (x + 1) * order, :, t * ez : (t + 1) * ez],
                    sems.at[len(copies)],
                )
            )
    for copy in copies:
        copy.start()
    for copy in copies:
        copy.wait()


def shards(counts, velocity, mask, scale):
    ex, ey, ez = mask.shape
    brick = Brick(ex, ey, ez)
    tile = (brick.rows, ez)
    f32 = jnp.float32
    whole = pl.BlockSpec(memory_space=pltpu.VMEM)
    remote = pl.BlockSpec(memory_space=pltpu.HBM)
    sems = pltpu.SemaphoreType.DMA
    lines = (order, order)
    strips = (order, order, ex * brick.pitch, ez)
    triples = len(list(itertools.combinations_with_replacement(range(order), 3)))
    pairs = [(order * ex * 3,), (2,)]
    for n in (6 * ey, 2 * ex, 2, 2 * ey, 2 * ex, 2, len(corners)):
        pairs += [(n,), (n,)]

    def vmem(*shape):
        return pltpu.VMEM(shape, f32)

    packed, part = pl.pallas_call(
        functools.partial(body, brick, counts),
        out_shape=(
            jax.ShapeDtypeStruct(strips, f32),
            jax.ShapeDtypeStruct(mask.shape, f32),
        ),
        in_specs=[remote] * 3,
        out_specs=(whole, whole),
        scratch_shapes=[
            vmem(3, *strips),
            pltpu.VMEM(mask.shape, jnp.int32),
            vmem(*scale.shape),
            vmem(3, order, *lines, *tile),
            vmem(3, order, *lines, *tile),
            vmem(2, 3, *lines, *tile),
            vmem(2, 3, *lines, *tile),
            vmem(2, *tile),
            vmem(2, *tile),
            vmem(2, 3, *lines, *tile),
            vmem(2, 2, *lines, *tile),
            vmem(order, *lines, *tile),
            vmem(triples, *tile),
            vmem(2, *lines, *tile),
            vmem(2, *lines, *tile),
            vmem(2, *tile),
            vmem(2, *tile),
            vmem(len(corners), *tile),
            vmem(len(corners), *tile),
        ]
        + [sems(shape) for shape in pairs],
        compiler_params=pltpu.CompilerParams(
            collective_id=0, has_side_effects=True, vmem_limit_bytes=32 << 20
        ),
    )(*[pltpu.with_memory_space_constraint(z, pltpu.HBM) for z in (velocity, mask, scale)])
    return pl.pallas_call(
        functools.partial(deliver, brick),
        out_shape=(
            jax.ShapeDtypeStruct(velocity.shape[1:], f32),
            jax.ShapeDtypeStruct(mask.shape, f32),
        ),
        in_specs=[whole] * 2,
        out_specs=(remote, remote),
        scratch_shapes=[sems((1 + ex * order,))],
        compiler_params=pltpu.CompilerParams(vmem_limit_bytes=16 << 20),
    )(packed, part)


def solution(mesh):
    counts = tuple(mesh.shape[name] for name in names)
    return jax.shard_map(
        functools.partial(shards, counts),
        mesh=mesh,
        in_specs=(P(None, "gx", "gy", "gz"), P("gx", "gy", "gz"), P("gx", "gy", "gz")),
        out_specs=(P("gx", "gy", "gz"), P("gx", "gy", "gz")),
        check_vma=False,
    )
```

```python
import functools
import itertools
import math

import jax
import jax.numpy as jnp
import numpy as np
from jax import lax
from jax.experimental import pallas as pl
from jax.experimental.pallas import tpu as pltpu
from jax.sharding import PartitionSpec as P

lift_factor = 10.0
time_step = 0.05
penalty = 4.0
half_lift = lift_factor * 0.5
order = 5
names = ("gx", "gy", "gz")
corners = [s for s in itertools.product((0, 1), repeat=3) if any(s)]
x_order = (0, 2, 1)


def lobatto_points():
    return np.array([-1.0, -math.sqrt(3.0 / 7.0), 0.0, math.sqrt(3.0 / 7.0), 1.0])


def lobatto_weights():
    return np.array([0.1, 49.0 / 90.0, 32.0 / 45.0, 49.0 / 90.0, 0.1])


def derivative_matrix():
    points = lobatto_points()
    scales = np.array(
        [np.prod([points[i] - points[k] for k in range(5) if k != i]) for i in range(5)]
    )
    result = np.zeros((5, 5))
    for i in range(5):
        for j in range(5):
            if i != j:
                result[i, j] = scales[i] / (scales[j] * (points[i] - points[j]))
        result[i, i] = -np.sum(result[i])
    return result


def eigen_value_table():
    return np.array([4.0 * math.sin(math.pi * k / 10.0) ** 2 for k in range(5)])


def hat_weight_table():
    points = lobatto_points()
    weights = lobatto_weights()
    return np.array([weights * (1.0 - points) / 2.0, weights * (1.0 + points) / 2.0])


def mix(coefs, terms):
    total = None
    for coef, term in zip(coefs, terms):
        if abs(coef) < 1e-12:
            continue
        piece = float(coef) * term
        total = piece if total is None else total + piece
    return total


def lifted_derivative(f, factor):
    d = derivative_matrix()
    d[0, 0] += half_lift
    d[4, 4] -= half_lift
    d = d * factor
    e1, e2 = f[0] + f[4], f[1] + f[3]
    o1, o2 = f[0] - f[4], f[1] - f[3]
    out = [None] * 5
    for i in range(2):
        even = mix(((d[i, 0] + d[i, 4]) / 2, (d[i, 1] + d[i, 3]) / 2, d[i, 2]), (e1, e2, f[2]))
        odd = mix(((d[i, 0] - d[i, 4]) / 2, (d[i, 1] - d[i, 3]) / 2), (o1, o2))
        out[i] = odd + even
        out[4 - i] = odd - even
    out[2] = mix((d[2, 0], d[2, 1]), (o1, o2))
    return out


cos18, cos54 = math.cos(math.pi * 0.1), math.cos(math.pi * 0.3)
cos36, cos72 = math.cos(math.pi * 0.2), math.cos(math.pi * 0.4)
even_gain = (cos36 + cos72) / 2
odd_ratio = cos54 / cos18
norm_squares = [0.2, 0.4 * cos18**2, 0.4, 0.4 * cos18**2, 0.4]


def to_modes(f):
    e1, e2 = f[0] + f[4], f[1] + f[3]
    o1, o2 = f[0] - f[4], f[1] - f[3]
    s = e1 + e2
    p = even_gain * (e1 - e2)
    q = 0.25 * s - f[2]
    return [s + f[2], o1 + odd_ratio * o2, p + q, odd_ratio * o1 - o2, p - q]


def from_modes(c):
    s, d = c[2] + c[4], c[2] - c[4]
    p = even_gain * s
    base = c[0] + 0.25 * d
    even = (base + p, base - p)
    odd = (c[1] + odd_ratio * c[3], odd_ratio * c[1] - c[3])
    return [even[0] + odd[0], even[1] + odd[1], c[0] - d, even[1] - odd[1], even[0] - odd[0]]


def at_line(a, l, m):
    return ((l, m), (m, l), (m, slice(None), l))[a]


def roll(x, shift, axis):
    size = x.shape[axis]
    shift = shift % size
    return x if shift == 0 else pltpu.roll(x, shift, axis)


class Brick:
    def __init__(self, ex, ey, ez):
        self.ex, self.ey, self.ez = ex, ey, ez
        self.rows = ex * ey
        self.ny = ey * order
        self.pitch = -(-self.ny // 8) * 8

    def iotas(self):
        row = lax.broadcasted_iota(jnp.int32, (self.rows, self.ez), 0)
        lane = lax.broadcasted_iota(jnp.int32, (self.rows, self.ez), 1)
        return row, lane

    def slots(self, a):
        return (self.ex, self.ey, self.ez)[a]

    def place(self, a):
        row, lane = self.iotas()
        return (row // self.ey, row % self.ey, lane)[a]

    def move(self, x, a, up):
        step = (self.ey, 1, 1)[a]
        return roll(x, step if up else -step, x.ndim - (1 if a == 2 else 2))

    def edge(self, a, up):
        return self.place(a) == (0 if up else self.slots(a) - 1)


def body(
    brick,
    counts,
    v_ref,
    mask_ref,
    scale_ref,
    out_ref,
    coarse_ref,
    raw,
    mask_buf,
    scale_buf,
    vel,
    conv,
    top_x,
    top2_x,
    far_x,
    far_y,
    send_z,
    far_z,
    shifted,
    gain,
    pres,
    inverse,
    far2_x,
    far2_y,
    send2_z,
    far2_z,
    send3,
    recv3,
    *sems,
):
    (load_sem, small_sem, sx, rx, sy, ry, sz, rz, s2x, r2x, s2y, r2y, s2z, r2z, s3, r3) = sems
    ex, ey, ez, rows, ny, pitch = brick.ex, brick.ey, brick.ez, brick.rows, brick.ny, brick.pitch
    me = [lax.axis_index(name) for name in names]

    def exists(shift):
        ok = None
        for a in range(3):
            if shift[a] > 0:
                one = me[a] < counts[a] - 1
            elif shift[a] < 0:
                one = me[a] > 0
            else:
                continue
            ok = one if ok is None else jnp.logical_and(ok, one)
        return ok

    def device(shift):
        return tuple(me[a] + shift[a] for a in range(3))

    unit = [tuple(int(a == b) for b in range(3)) for a in range(3)]

    def toward(a, s):
        return tuple((1 - 2 * s) * u for u in unit[a])

    partners = [toward(a, s) for a in range(3) for s in range(2)]
    greeted = partners + [(-1, -1, -1)]
    awaited = partners + [(1, 1, 1)]
    barrier = pltpu.get_barrier_semaphore()
    for shift in greeted:

        @pl.when(exists(shift))
        def _():
            pl.semaphore_signal(
                barrier, inc=1, device_id=device(shift), device_id_type=pl.DeviceIdType.MESH
            )

    loads = {}
    for c in x_order:
        for x in range(ex):
            for t in range(order):
                loads[c, x, t] = pltpu.make_async_copy(
                    v_ref.at[c, x * order : (x + 1) * order, :, t * ez : (t + 1) * ez],
                    raw.at[c, :, t, x * pitch : x * pitch + ny],
                    load_sem.at[c],
                )
                loads[c, x, t].start()
    small = [
        pltpu.make_async_copy(mask_ref, mask_buf, small_sem.at[0]),
        pltpu.make_async_copy(scale_ref, scale_buf, small_sem.at[1]),
    ]
    for copy in small:
        copy.start()

    class Group:
        def __init__(self, shift, pairs, ssem, rsem, dst, whole=None):
            self.to, self.source = exists(shift), exists(tuple(-x for x in shift))
            self.dst = dst
            self.copies = [self.copy(src, to, ssem, rsem, shift) for src, to in pairs]
            self.all = self.copies[0] if whole is None else self.copy(whole, whole, ssem, rsem, shift)

        def copy(self, src, dst, ssem, rsem, shift):
            return pltpu.make_async_remote_copy(
                src_ref=src,
                dst_ref=dst,
                send_sem=ssem,
                recv_sem=rsem,
                device_id=device(shift),
                device_id_type=pl.DeviceIdType.MESH,
            )

        def start(self):
            @pl.when(self.to)
            def _():
                for copy in self.copies:
                    copy.start()

        def clear(self):
            @pl.when(jnp.logical_not(self.source))
            def _():
                self.dst[...] = jnp.zeros_like(self.dst)

        def arrive(self):
            @pl.when(self.source)
            def _():
                self.all.wait_recv()

        def finish(self):
            @pl.when(self.to)
            def _():
                self.all.wait_send()

    def y_rows(s):
        return [
            (x * ey + ey - 1, x * ey) if s == 0 else (x * ey, x * ey + ey - 1) for x in range(ex)
        ]

    def face(s):
        return order - 1 if s == 0 else 0

    round1x, round1, round2, round3 = {}, {}, {}, {}
    for s in range(2):
        for c in range(3):
            n = c * 2 + s
            src = top_x.at[c] if s == 0 else vel.at[c, 0]
            round1x[c, s] = Group(
                toward(0, s),
                [(src.at[:, :, 0:ey], far_x.at[s, c, :, :, 0:ey])],
                sx.at[n],
                rx.at[n],
                far_x.at[s, c],
            )
        round1[1, s] = Group(
            toward(1, s),
            [
                (vel.at[:, :, face(s), :, src], far_y.at[s, :, :, :, dst])
                for src, dst in y_rows(s)
            ],
            sy.at[s],
            ry.at[s],
            far_y.at[s],
            far_y.at[s, :, :, :, 0:ex],
        )
        round1[2, s] = Group(
            toward(2, s), [(send_z.at[s], far_z.at[s])], sz.at[s], rz.at[s], far_z.at[s]
        )
        src = top2_x if s == 0 else conv.at[0, 0]
        round2[0, s] = Group(
            toward(0, s),
            [(src.at[:, :, 0:ey], far2_x.at[s, :, :, 0:ey])],
            s2x.at[s],
            r2x.at[s],
            far2_x.at[s],
        )
        round2[1, s] = Group(
            toward(1, s),
            [
                (conv.at[1, :, face(s), :, src], far2_y.at[s, :, :, dst])
                for src, dst in y_rows(s)
            ],
            s2y.at[s],
            r2y.at[s],
            far2_y.at[s],
            far2_y.at[s, :, :, 0:ex],
        )
        round2[2, s] = Group(
            toward(2, s), [(send2_z.at[s], far2_z.at[s])], s2z.at[s], r2z.at[s], far2_z.at[s]
        )
    for n, shift in enumerate(corners):
        round3[n] = Group(shift, [(send3.at[n], recv3.at[n])], s3.at[n], r3.at[n], recv3.at[n])

    def each(groups, act):
        for key in groups:
            getattr(groups[key], act)()

    def pick(groups, a):
        return {key: groups[key] for key in groups if key[0] == a}

    row, lane = brick.iotas()
    spread = pow(order, -1, ez)
    turn = pow(ez, -1, order)
    phase = (turn * lane) % order
    bits = [(phase & bit) != 0 for bit in (1, 2, 4)]
    place_x = brick.place(0)

    def permute(x, index):
        return jnp.take_along_axis(x, index, axis=1, mode="promise_in_bounds")

    def barrel(tiles, sign):
        for bit, on in zip((1, 2, 4), bits):
            tiles = [jnp.where(on, tiles[(m - sign * bit) % order], tiles[m]) for m in range(order)]
        return tiles

    def pack_entry(total, tile, n, s):
        start = ez - 1 if s == 0 else 0
        return jnp.where(lane == n, roll(tile, n - start, 1), total)

    def unpack_entry(packed, n, s):
        return roll(packed, (0 if s == 0 else ez - 1) - n, 1)

    zero = jnp.zeros((rows, ez), jnp.float32)

    packs = [zero, zero]
    for c in x_order:
        landed = raw.at[c, :, :, 0 : ex * ny]
        pltpu.make_async_copy(landed, landed, load_sem.at[c]).wait()
        for i in (4, 0, 1, 2, 3):
            merged = []
            for j in range(order):
                natural = []
                for t in range(order):
                    tile = None
                    for x in range(ex):
                        start = j + x * (pitch - ny)
                        part = raw[c, i, t, pl.ds(start, rows, stride=order), :]
                        tile = part if x == 0 else jnp.where(place_x == x, part, tile)
                    natural.append(tile)
                merged.append(barrel(natural, 1))
            for k in range(order):
                index = (lane * order + k) % ez
                for j in range(order):
                    tile = permute(merged[j][(turn * k) % order], index)
                    vel[c, i, j, k] = tile
                    if i == order - 1:
                        top_x[c, j, k] = roll(tile, ey - rows, 0)
                    n = (c * order + i) * order + j
                    for s in range(2):
                        if k == face(s):
                            packs[s] = pack_entry(packs[s], tile, n, s)
        if c == x_order[0]:
            pl.semaphore_wait(barrier, sum(exists(shift).astype(jnp.int32) for shift in awaited))
        each(pick(round1x, c), "start")
    for s in range(2):
        send_z[s] = packs[s]
    each(round1, "start")

    each(round1x, "clear")
    each(round1, "clear")
    each(round2, "clear")
    each(round3, "clear")

    def inner_axis(a):
        def run(m, carry):
            normal = [vel[(a,) + at_line(a, l, m)] for l in range(order)]
            for c in range(3):
                if c == a:
                    moved = normal
                else:
                    moved = [vel[(c,) + at_line(a, l, m)] for l in range(order)]
                out = lifted_derivative([n * w for n, w in zip(normal, moved)], -time_step)
                for l in range(order):
                    where = (c,) + at_line(a, l, m)
                    conv[where] = (moved[l] if a == 0 else conv[where]) + out[l]
                if a == 2:
                    for s in range(2):
                        shifted[s, c, m] = brick.move(moved[face(s)], 2, s == 0)
            return carry

        lax.fori_loop(0, order, run, 0)

    for a in range(3):
        inner_axis(a)

    for copy in small:
        copy.wait()
    solid = jnp.concatenate([mask_buf[x] for x in range(ex)], axis=0).astype(jnp.float32)
    scale = jnp.concatenate([scale_buf[x] for x in range(ex)], axis=0)
    fluid = 1.0 / (1.0 + penalty * solid)

    eigen = eigen_value_table()
    slot_of = {}
    for key in itertools.combinations_with_replacement(range(order), 3):
        slot_of[key] = len(slot_of)
        size = float(np.prod([norm_squares[k] for k in key]))
        inverse[slot_of[key]] = 1.0 / (scale * float(sum(eigen[k] for k in key) / size) + 1.0 / size)

    edges = [[brick.edge(a, s == 0) for s in range(2)] for a in range(3)]

    def from_x(far, s):
        return far if s == 0 else roll(far, rows - ey, far.ndim - 2)

    def near(a, s, c, m):
        other = face(s)
        if a == 2:
            tiles = [
                jnp.where(
                    edges[2][s],
                    unpack_entry(far_z[s], (c * order + m) * order + q, s),
                    shifted[s, c, m, q],
                )
                for q in range(order)
            ]
            return jnp.stack(tiles)
        far = from_x(far_x[s, c, m], s) if a == 0 else far_y[s, c, m]
        return jnp.where(edges[a][s], far, brick.move(vel[(c,) + at_line(a, other, m)], a, s == 0))

    step_lift = time_step * half_lift

    def face_terms(a, components):
        for s in range(2):
            own = order - 1 - face(s)
            for m in range(order):
                outside = None
                if a > 0 or components[0] == 0:
                    normal = vel[(a,) + at_line(a, own, m)]
                    outside = near(a, s, a, m)
                    down = step_lift * jnp.maximum(jnp.abs(normal), jnp.abs(outside))
                    flow = step_lift * outside
                    across = down + flow if s == 0 else down - flow
                    if a == 0:
                        gain[s, 0, m] = across
                        gain[s, 1, m] = down
                else:
                    across, down = gain[s, 0, m], gain[s, 1, m]
                for c in components:
                    moved_out = outside if c == a else near(a, s, c, m)
                    where = (c,) + at_line(a, own, m)
                    conv[where] = conv[where] + (across * moved_out - down * vel[where])

    def advance(c, i):
        conv[c, i] = conv[c, i] * fluid

    for a in (1, 2):
        each(pick(round1, a), "arrive")
        face_terms(a, (0, 1, 2))
    for c in range(3):
        for i in range(1, order - 1):
            advance(c, i)

    def diverge(a, lines):
        for m in lines:
            out = lifted_derivative([conv[(a,) + at_line(a, l, m)] for l in range(order)], -1.0)
            for l in range(order):
                where = at_line(a, l, m)
                pres[where] = out[l] if a == 0 else pres[where] + out[l]

    packs2 = [zero, zero]

    def pack2(i, packs2):
        for j in range(order):
            for s in range(2):
                packs2[s] = pack_entry(packs2[s], conv[2, i, j, face(s)], i * order + j, s)

    for c in x_order:
        each(pick(round1x, c), "arrive")
        face_terms(0, (c,))
        advance(c, 0)
        advance(c, order - 1)
        if c == 0:
            for j in range(order):
                for k in range(order):
                    top2_x[j, k] = roll(conv[0, order - 1, j, k], ey - rows, 0)
        if c == 2:
            pack2(0, packs2)
            pack2(order - 1, packs2)
            for s in range(2):
                send2_z[s] = packs2[s]
        each(pick(round2, c), "start")
        if c == 0:
            diverge(0, range(order))
            for i in range(1, order - 1):
                pack2(i, packs2)
            diverge(1, range(1, order - 1))
            diverge(2, range(1, order - 1))
        else:
            diverge(c, (0, order - 1))

    hats = hat_weight_table()
    slopes = lobatto_weights() / 2

    def hat_pair(lines):
        e1, e2 = lines[0] + lines[4], lines[1] + lines[3]
        whole_sum = mix((hats[0, 0] + hats[0, 4], hats[0, 1] + hats[0, 3], hats[0, 2] * 2), (e1, e2, lines[2]))
        d1, d2 = lines[4] - lines[0], lines[3] - lines[1]
        gap = mix((hats[0, 0] - hats[0, 4], hats[0, 1] - hats[0, 3]), (d1, d2))
        return (0.5 * (whole_sum - gap), 0.5 * (whole_sum + gap))

    def plane(get):
        along = [hat_pair([get(p, q) for q in range(order)]) for p in range(order)]
        return [
            list(pair)
            for pair in zip(*[hat_pair([along[p][b] for p in range(order)]) for b in range(2)])
        ]

    def index_of(a, l, p, q):
        return ((l, p, q), (p, l, q), (p, q, l))[a]

    parts = {}
    for a in range(3):

        def slope(p, q):
            f = [conv[(a,) + index_of(a, l, p, q)] for l in range(order)]
            return mix(slopes[:3], (f[0] + f[4], f[1] + f[3], f[2]))

        inner = plane(slope)
        ends = plane(lambda p, q: conv[(a,) + index_of(a, 0, p, q)])
        open_end = jnp.where(jnp.logical_and(edges[a][0], me[a] == 0), 0.5, 0.0)
        for p in range(2):
            for q in range(2):
                for b in range(2):
                    key = index_of(a, b, p, q)
                    piece = inner[p][q] if b == 1 else open_end * ends[p][q] - inner[p][q]
                    parts[key] = parts[key] + piece if key in parts else piece
    for a in (2, 1, 0):
        edge = edges[a][0]
        merged = {}
        for key in parts:
            if key[a] == 1:
                continue
            upper = key[:a] + (1,) + key[a + 1 :]
            moved = brick.move(parts[upper], a, True)
            if a == 1:
                moved = jnp.where(edge, roll(parts[upper], 1 - ey, 0), moved)
            merged[key] = parts[key] + jnp.where(edge, 0.0, moved)
            merged[upper] = jnp.where(edge, moved, 0.0)
        parts = merged
    for n, shift in enumerate(corners):
        send3[n] = parts[shift]
    each(round3, "start")

    each(round1x, "finish")
    each(round1, "finish")

    for a in (0, 2, 1):
        each(pick(round2, a), "arrive")
        for s in range(2):
            own = order - 1 - face(s)
            for m in range(order):
                line = conv[(a,) + at_line(a, face(s), m)]
                if a == 2:
                    far = jnp.stack(
                        [unpack_entry(far2_z[s], m * order + q, s) for q in range(order)]
                    )
                else:
                    far = from_x(far2_x[s, m], s) if a == 0 else far2_y[s, m]
                side = jnp.where(edges[a][s], far, brick.move(line, a, s == 0))
                where = at_line(a, own, m)
                if s == 0:
                    pres[where] = pres[where] + half_lift * side
                else:
                    pres[where] = pres[where] - half_lift * side

    def forward(i, carry):
        slab = to_modes([pres[i, j] for j in range(order)])
        for j in range(order):
            out = to_modes([slab[j][k] for k in range(order)])
            for k in range(order):
                pres[i, j, k] = out[k]
        return carry

    lax.fori_loop(0, order, forward, 0)

    for j in range(order):
        for k in range(order):
            modes = to_modes([pres[i, j, k] for i in range(order)])
            modes = [
                modes[i] * inverse[slot_of[tuple(sorted((i, j, k)))]] for i in range(order)
            ]
            out = from_modes(modes)
            for i in range(order):
                pres[i, j, k] = out[i]

    for i in range(order):
        slab = from_modes([pres[i, j] for j in range(order)])
        lines = [from_modes([slab[j][k] for k in range(order)]) for j in range(order)]
        mixed = [[None] * order for _ in range(order)]
        for k in range(order):
            index = ((lane + (ez - k)) * spread) % ez
            for j in range(order):
                mixed[j][(turn * k) % order] = permute(lines[j][k], index)
        for j in range(order):
            natural = barrel(mixed[j], -1)
            for t in range(order):
                for x in range(ex):
                    out_ref[i, t, pl.ds(x * pitch + j, ey, stride=order), :] = natural[t][
                        x * ey : (x + 1) * ey
                    ]

    each(round2, "finish")
    each(round3, "arrive")
    total = parts[(0, 0, 0)]
    for n in range(len(corners)):
        total = total + recv3[n]
    for x in range(ex):
        coarse_ref[x] = total[x * ey : (x + 1) * ey]
    each(round3, "finish")


def deliver(brick, packed_ref, part_ref, smooth_ref, coarse_ref, sems):
    ez, ny, pitch = brick.ez, brick.ny, brick.pitch
    copies = [pltpu.make_async_copy(part_ref, coarse_ref, sems.at[0])]
    for x in range(brick.ex):
        for t in range(order):
            copies.append(
                pltpu.make_async_copy(
                    packed_ref.at[:, t, x * pitch : x * pitch + ny],
                    smooth_ref.at[x * order : (x + 1) * order, :, t * ez : (t + 1) * ez],
                    sems.at[len(copies)],
                )
            )
    for copy in copies:
        copy.start()
    for copy in copies:
        copy.wait()


def shards(counts, velocity, mask, scale):
    ex, ey, ez = mask.shape
    brick = Brick(ex, ey, ez)
    tile = (brick.rows, ez)
    f32 = jnp.float32
    whole = pl.BlockSpec(memory_space=pltpu.VMEM)
    remote = pl.BlockSpec(memory_space=pltpu.HBM)
    sems = pltpu.SemaphoreType.DMA
    lines = (order, order)
    strips = (order, order, ex * brick.pitch, ez)
    triples = len(list(itertools.combinations_with_replacement(range(order), 3)))
    pairs = [(3,), (2,)]
    for n in (6, 2, 2, 2, 2, 2, len(corners)):
        pairs += [(n,), (n,)]

    def vmem(*shape):
        return pltpu.VMEM(shape, f32)

    packed, part = pl.pallas_call(
        functools.partial(body, brick, counts),
        out_shape=(
            jax.ShapeDtypeStruct(strips, f32),
            jax.ShapeDtypeStruct(mask.shape, f32),
        ),
        in_specs=[remote] * 3,
        out_specs=(whole, whole),
        scratch_shapes=[
            vmem(3, *strips),
            pltpu.VMEM(mask.shape, jnp.int32),
            vmem(*scale.shape),
            vmem(3, order, *lines, *tile),
            vmem(3, order, *lines, *tile),
            vmem(3, *lines, *tile),
            vmem(*lines, *tile),
            vmem(2, 3, *lines, *tile),
            vmem(2, 3, *lines, *tile),
            vmem(2, *tile),
            vmem(2, *tile),
            vmem(2, 3, *lines, *tile),
            vmem(2, 2, *lines, *tile),
            vmem(order, *lines, *tile),
            vmem(triples, *tile),
            vmem(2, *lines, *tile),
            vmem(2, *lines, *tile),
            vmem(2, *tile),
            vmem(2, *tile),
            vmem(len(corners), *tile),
            vmem(len(corners), *tile),
        ]
        + [sems(shape) for shape in pairs],
        compiler_params=pltpu.CompilerParams(
            collective_id=0, has_side_effects=True, vmem_limit_bytes=32 << 20
        ),
    )(*[pltpu.with_memory_space_constraint(z, pltpu.HBM) for z in (velocity, mask, scale)])
    return pl.pallas_call(
        functools.partial(deliver, brick),
        out_shape=(
            jax.ShapeDtypeStruct(velocity.shape[1:], f32),
            jax.ShapeDtypeStruct(mask.shape, f32),
        ),
        in_specs=[whole] * 2,
        out_specs=(remote, remote),
        scratch_shapes=[sems((1 + ex * order,))],
        compiler_params=pltpu.CompilerParams(vmem_limit_bytes=16 << 20),
    )(packed, part)


def solution(mesh):
    counts = tuple(mesh.shape[name] for name in names)
    return jax.shard_map(
        functools.partial(shards, counts),
        mesh=mesh,
        in_specs=(P(None, "gx", "gy", "gz"), P("gx", "gy", "gz"), P("gx", "gy", "gz")),
        out_specs=(P("gx", "gy", "gz"), P("gx", "gy", "gz")),
        check_vma=False,
    )
```

```python
import functools
import itertools
import math

import jax
import jax.numpy as jnp
import numpy as np
from jax import lax
from jax.experimental import pallas as pl
from jax.experimental.pallas import tpu as pltpu
from jax.sharding import PartitionSpec as P

lift_factor = 10.0
time_step = 0.05
penalty = 4.0
half_lift = lift_factor * 0.5
order = 5
names = ("gx", "gy", "gz")
corners = [s for s in itertools.product((0, 1), repeat=3) if any(s)]
x_order = (0, 2, 1)


def lobatto_points():
    return np.array([-1.0, -math.sqrt(3.0 / 7.0), 0.0, math.sqrt(3.0 / 7.0), 1.0])


def lobatto_weights():
    return np.array([0.1, 49.0 / 90.0, 32.0 / 45.0, 49.0 / 90.0, 0.1])


def derivative_matrix():
    points = lobatto_points()
    scales = np.array(
        [np.prod([points[i] - points[k] for k in range(5) if k != i]) for i in range(5)]
    )
    result = np.zeros((5, 5))
    for i in range(5):
        for j in range(5):
            if i != j:
                result[i, j] = scales[i] / (scales[j] * (points[i] - points[j]))
        result[i, i] = -np.sum(result[i])
    return result


def eigen_value_table():
    return np.array([4.0 * math.sin(math.pi * k / 10.0) ** 2 for k in range(5)])


def hat_weight_table():
    points = lobatto_points()
    weights = lobatto_weights()
    return np.array([weights * (1.0 - points) / 2.0, weights * (1.0 + points) / 2.0])


def mix(coefs, terms):
    total = None
    for coef, term in zip(coefs, terms):
        if abs(coef) < 1e-12:
            continue
        piece = float(coef) * term
        total = piece if total is None else total + piece
    return total


def lifted_derivative(f, factor):
    d = derivative_matrix()
    d[0, 0] += half_lift
    d[4, 4] -= half_lift
    d = d * factor
    e1, e2 = f[0] + f[4], f[1] + f[3]
    o1, o2 = f[0] - f[4], f[1] - f[3]
    out = [None] * 5
    for i in range(2):
        even = mix(((d[i, 0] + d[i, 4]) / 2, (d[i, 1] + d[i, 3]) / 2, d[i, 2]), (e1, e2, f[2]))
        odd = mix(((d[i, 0] - d[i, 4]) / 2, (d[i, 1] - d[i, 3]) / 2), (o1, o2))
        out[i] = odd + even
        out[4 - i] = odd - even
    out[2] = mix((d[2, 0], d[2, 1]), (o1, o2))
    return out


cos18, cos54 = math.cos(math.pi * 0.1), math.cos(math.pi * 0.3)
cos36, cos72 = math.cos(math.pi * 0.2), math.cos(math.pi * 0.4)
even_gain = (cos36 + cos72) / 2
odd_ratio = cos54 / cos18
norm_squares = [0.2, 0.4 * cos18**2, 0.4, 0.4 * cos18**2, 0.4]


def to_modes(f):
    e1, e2 = f[0] + f[4], f[1] + f[3]
    o1, o2 = f[0] - f[4], f[1] - f[3]
    s = e1 + e2
    p = even_gain * (e1 - e2)
    q = 0.25 * s - f[2]
    return [s + f[2], o1 + odd_ratio * o2, p + q, odd_ratio * o1 - o2, p - q]


def from_modes(c):
    s, d = c[2] + c[4], c[2] - c[4]
    p = even_gain * s
    base = c[0] + 0.25 * d
    even = (base + p, base - p)
    odd = (c[1] + odd_ratio * c[3], odd_ratio * c[1] - c[3])
    return [even[0] + odd[0], even[1] + odd[1], c[0] - d, even[1] - odd[1], even[0] - odd[0]]


def roll(x, shift, axis):
    size = x.shape[axis]
    shift = shift % size
    return x if shift == 0 else pltpu.roll(x, shift, axis)


class Brick:
    def __init__(self, ex, ey, ez):
        self.ex, self.ey, self.ez = ex, ey, ez
        self.rows = ex * ey
        self.ny = ey * order
        self.pitch = -(-self.ny // 8) * 8

    def iotas(self):
        row = lax.broadcasted_iota(jnp.int32, (self.rows, self.ez), 0)
        lane = lax.broadcasted_iota(jnp.int32, (self.rows, self.ez), 1)
        return row, lane

    def slots(self, a):
        return (self.ex, self.ey, self.ez)[a]

    def place(self, a):
        row, lane = self.iotas()
        return (row // self.ey, row % self.ey, lane)[a]

    def move(self, x, a, up):
        step = (self.ey, 1, 1)[a]
        return roll(x, step if up else -step, x.ndim - (1 if a == 2 else 2))

    def edge(self, a, up):
        return self.place(a) == (0 if up else self.slots(a) - 1)


def body(
    brick,
    counts,
    v_ref,
    mask_ref,
    scale_ref,
    out_ref,
    coarse_ref,
    raw,
    mask_buf,
    scale_buf,
    vel,
    conv,
    strip_x,
    raw_y,
    far_x,
    far_y,
    send_z,
    far_z,
    shifted,
    gain,
    pres,
    inverse,
    top2_x,
    far2_x,
    far2_y,
    send2_z,
    far2_z,
    send3,
    recv3,
    *sems,
):
    (load_sem, small_sem, sx, rx, sy, ry, sz, rz, s2x, r2x, s2y, r2y, s2z, r2z, s3, r3) = sems
    ex, ey, ez, rows, ny, pitch = brick.ex, brick.ey, brick.ez, brick.rows, brick.ny, brick.pitch
    me = [lax.axis_index(name) for name in names]
    ends, middle = (0, order - 1), tuple(range(1, order - 1))

    def exists(shift):
        ok = None
        for a in range(3):
            if shift[a] > 0:
                one = me[a] < counts[a] - 1
            elif shift[a] < 0:
                one = me[a] > 0
            else:
                continue
            ok = one if ok is None else jnp.logical_and(ok, one)
        return ok

    def device(shift):
        return tuple(me[a] + shift[a] for a in range(3))

    unit = [tuple(int(a == b) for b in range(3)) for a in range(3)]

    def toward(a, s):
        return tuple((1 - 2 * s) * u for u in unit[a])

    partners = [toward(a, s) for a in range(3) for s in range(2)]
    greeted = partners + [(-1, -1, -1)]
    awaited = partners + [(1, 1, 1)]
    barrier = pltpu.get_barrier_semaphore()
    for shift in greeted:

        @pl.when(exists(shift))
        def _():
            pl.semaphore_signal(
                barrier, inc=1, device_id=device(shift), device_id_type=pl.DeviceIdType.MESH
            )

    for t in ends + middle:
        for x in range(ex):
            pltpu.make_async_copy(
                v_ref.at[:, x * order : (x + 1) * order, :, t * ez : (t + 1) * ez],
                raw.at[:, :, t, x * pitch : x * pitch + ny],
                load_sem.at[0 if t in ends else 1],
            ).start()
    small = [
        pltpu.make_async_copy(mask_ref, mask_buf, small_sem.at[0]),
        pltpu.make_async_copy(scale_ref, scale_buf, small_sem.at[1]),
    ]
    for copy in small:
        copy.start()

    def loaded(group):
        landed = raw.at[:, :, 0 : (2, order - 2)[group], 0 : ex * ny]
        pltpu.make_async_copy(landed, landed, load_sem.at[group]).wait()

    class Group:
        def __init__(self, shift, pairs, ssem, rsem, dst, whole=None):
            self.to, self.source = exists(shift), exists(tuple(-x for x in shift))
            self.dst = dst
            self.copies = [self.copy(src, to, ssem, rsem, shift) for src, to in pairs]
            self.all = self.copies[0] if whole is None else self.copy(whole, whole, ssem, rsem, shift)

        def copy(self, src, dst, ssem, rsem, shift):
            return pltpu.make_async_remote_copy(
                src_ref=src,
                dst_ref=dst,
                send_sem=ssem,
                recv_sem=rsem,
                device_id=device(shift),
                device_id_type=pl.DeviceIdType.MESH,
            )

        def start(self):
            @pl.when(self.to)
            def _():
                for copy in self.copies:
                    copy.start()

        def clear(self):
            @pl.when(jnp.logical_not(self.source))
            def _():
                self.dst[...] = jnp.zeros_like(self.dst)

        def arrive(self):
            @pl.when(self.source)
            def _():
                self.all.wait_recv()

        def finish(self):
            @pl.when(self.to)
            def _():
                self.all.wait_send()

    def y_rows(s):
        return [
            (x * ey + ey - 1, x * ey) if s == 0 else (x * ey, x * ey + ey - 1) for x in range(ex)
        ]

    def face(s):
        return order - 1 if s == 0 else 0

    round1x, round1, round2, round3 = {}, {}, {}, {}
    for s in range(2):
        for c in range(3):
            n = c * 2 + s
            x, to = (ex - 1, 0) if s == 0 else (0, ex - 1)
            round1x[c, s] = Group(
                toward(0, s),
                [
                    (
                        raw.at[c, face(s), :, x * pitch : x * pitch + ny],
                        strip_x.at[c, :, to * pitch : to * pitch + ny],
                    )
                ],
                sx.at[n],
                rx.at[n],
                None,
            )
        line = ny - 1 if s == 0 else 0
        round1[1, s] = Group(
            toward(1, s),
            [
                (raw.at[:, :, :, x * pitch + line], raw_y.at[:, :, :, dst])
                for x, (_, dst) in enumerate(y_rows(s))
            ],
            sy.at[s],
            ry.at[s],
            None,
            raw_y.at[:, :, :, 0:ex],
        )
        round1[2, s] = Group(
            toward(2, s), [(send_z.at[s], far_z.at[s])], sz.at[s], rz.at[s], None
        )
        src = top2_x if s == 0 else conv.at[0, 0]
        round2[0, s] = Group(
            toward(0, s),
            [(src.at[:, :, 0:ey], far2_x.at[s, :, :, 0:ey])],
            s2x.at[s],
            r2x.at[s],
            far2_x.at[s],
        )
        round2[1, s] = Group(
            toward(1, s),
            [
                (conv.at[1, :, face(s), :, src], far2_y.at[s, :, :, dst])
                for src, dst in y_rows(s)
            ],
            s2y.at[s],
            r2y.at[s],
            far2_y.at[s],
            far2_y.at[s, :, :, 0:ex],
        )
        round2[2, s] = Group(
            toward(2, s), [(send2_z.at[s], far2_z.at[s])], s2z.at[s], r2z.at[s], far2_z.at[s]
        )
    for n, shift in enumerate(corners):
        round3[n] = Group(shift, [(send3.at[n], recv3.at[n])], s3.at[n], r3.at[n], recv3.at[n])

    def each(groups, act):
        for key in groups:
            getattr(groups[key], act)()

    def pick(groups, a):
        return {key: groups[key] for key in groups if key[0] == a}

    row, lane = brick.iotas()
    spread = pow(order, -1, ez)
    turn = pow(ez, -1, order)
    phase = (turn * lane) % order
    bits = [(phase & bit) != 0 for bit in (1, 2, 4)]
    place_x = brick.place(0)
    edges = [[brick.edge(a, s == 0) for s in range(2)] for a in range(3)]
    zero = jnp.zeros((rows, ez), jnp.float32)

    def known(a):
        here = [jnp.logical_and(edges[a][s], exists(toward(a, 1 - s))) for s in range(2)]
        return jnp.logical_or(*here)

    def permute(x, index):
        return jnp.take_along_axis(x, index, axis=1, mode="promise_in_bounds")

    def barrel(tiles, sign):
        for bit, on in zip((1, 2, 4), bits):
            tiles = [jnp.where(on, tiles[(m - sign * bit) % order], tiles[m]) for m in range(order)]
        return tiles

    def split_index(k):
        return (lane * order + k) % ez

    def pack_entry(total, tile, n, s):
        start = ez - 1 if s == 0 else 0
        return jnp.where(lane == n, roll(tile, n - start, 1), total)

    def unpack_entry(packed, n, s):
        return roll(packed, (0 if s == 0 else ez - 1) - n, 1)

    def fetch(strip, j):
        tile = None
        for x in range(ex):
            part = strip[pl.ds(j + x * (pitch - ny), rows, stride=order), :]
            tile = part if x == 0 else jnp.where(place_x == x, part, tile)
        return tile

    loaded(0)
    for s in range(2):
        packs = zero
        for n in range(3 * order * order):
            c, i, j = n // order**2, n // order % order, n % order
            packs = pack_entry(packs, fetch(raw.at[c, i, face(s)], j), n, s)
        send_z[s] = packs

    loaded(1)
    pl.semaphore_wait(barrier, sum(exists(shift).astype(jnp.int32) for shift in awaited))
    each(pick(round1x, x_order[0]), "start")
    each(round1, "start")
    for c in x_order[1:]:
        each(pick(round1x, c), "start")

    def gather(c, i):
        for j in range(order):
            merged = barrel([fetch(raw.at[c, i, t], j) for t in range(order)], 1)
            for k in range(order):
                vel[c, i, j, k] = merged[(turn * k) % order]

    def scatter(c, k):
        for i in range(order):
            for j in range(order):
                vel[c, i, j, k] = permute(vel[c, i, j, k], split_index(k))

    for i in range(order):
        gather(x_order[0], i)
    for n, c in enumerate(x_order):
        for k in range(order):
            scatter(c, k)
            if n < 2:
                gather(x_order[n + 1], k)

    each(round2, "clear")
    each(round3, "clear")

    def node(a, l, p, q):
        return ((l, p, q), (p, l, q), (p, q, l))[a]

    def lines(a, c, wanted):
        pairs = itertools.product(range(order), repeat=2)
        return [pq for pq in pairs if a == c or node(a, 0, *pq)[c] in wanted]

    def inner(c, wanted):
        for a in (c,) + tuple(b for b in range(3) if b != c):
            for p, q in lines(a, c, wanted):
                normal = [vel[(a,) + node(a, l, p, q)] for l in range(order)]
                moved = normal
                if a != c:
                    moved = [vel[(c,) + node(a, l, p, q)] for l in range(order)]
                out = lifted_derivative([n * w for n, w in zip(normal, moved)], -time_step)
                for l in wanted if a == c else range(order):
                    where = (c,) + node(a, l, p, q)
                    conv[where] = (moved[l] if a == c else conv[where]) + out[l]

    for c in x_order:
        inner(c, ends)
    for s in range(2):
        for c in range(3):
            for p in range(order):
                for q in range(order):
                    shifted[s, c, p, q] = brick.move(vel[c, p, q, face(s)], 2, s == 0)

    for copy in small:
        copy.wait()
    solid = jnp.concatenate([mask_buf[x] for x in range(ex)], axis=0).astype(jnp.float32)
    scale = jnp.concatenate([scale_buf[x] for x in range(ex)], axis=0)
    fluid = 1.0 / (1.0 + penalty * solid)

    def near(a, s, c, p, q):
        if a == 2:
            far = unpack_entry(far_z[s], (c * order + p) * order + q, s)
            far = jnp.where(exists(toward(2, 1 - s)), far, zero)
            return jnp.where(edges[2][s], far, shifted[s, c, p, q])
        far = far_x[c, p, q] if a == 0 else far_y[c, p, q]
        inside = brick.move(vel[(c,) + node(a, face(s), p, q)], a, s == 0)
        return jnp.where(edges[a][s], far, inside)

    step_lift = time_step * half_lift

    def face_terms(a, c, wanted):
        for s in range(2):
            own = order - 1 - face(s)
            for p, q in lines(a, c, wanted):
                where = (c,) + node(a, own, p, q)
                moved, moved_out = vel[where], near(a, s, c, p, q)
                if a == c:
                    down = step_lift * jnp.maximum(jnp.abs(moved), jnp.abs(moved_out))
                    flow = step_lift * moved_out
                    across = down + flow if s == 0 else down - flow
                    gain[a, s, 0, p, q] = across
                    gain[a, s, 1, p, q] = down
                else:
                    across, down = gain[a, s, 0, p, q], gain[a, s, 1, p, q]
                conv[where] = conv[where] + (across * moved_out - down * moved)

    def advance(c, wanted):
        for l in wanted:
            for p in range(order):
                for q in range(order):
                    where = (c,) + node(c, l, p, q)
                    conv[where] = conv[where] * fluid

    each(pick(round1, 2), "arrive")
    for c in (2, 0, 1):
        face_terms(2, c, ends)

    each(pick(round1, 1), "arrive")
    valid = known(1)
    for i in range(order):
        mixed = {}
        for c in range(3):
            natural = [
                jnp.where(valid, raw_y[c, i, t], zero) for t in range(order)
            ]
            mixed[c] = barrel(natural, 1)
        for k in range(order):
            for c in range(3):
                far_y[c, i, k] = permute(mixed[c][(turn * k) % order], split_index(k))
    for c in (1, 0, 2):
        face_terms(1, c, ends)

    valid_x = known(0)
    for c in x_order:
        each(pick(round1x, c), "arrive")
        mixed = []
        for j in range(order):
            natural = [
                jnp.where(valid_x, fetch(strip_x.at[c, t], j), zero) for t in range(order)
            ]
            mixed.append(barrel(natural, 1))
        for k in range(order):
            for j in range(order):
                far_x[c, j, k] = permute(mixed[j][(turn * k) % order], split_index(k))
        face_terms(0, c, ends)
        advance(c, ends)
        if c == 0:
            for j in range(order):
                for k in range(order):
                    top2_x[j, k] = roll(conv[0, order - 1, j, k], ey - rows, 0)
        if c == 2:
            for s in range(2):
                packs = zero
                for n in range(order * order):
                    packs = pack_entry(packs, conv[2, n // order, n % order, face(s)], n, s)
                send2_z[s] = packs
        each(pick(round2, c), "start")

    for c in range(3):
        inner(c, middle)
        for a in range(3):
            if a != c:
                face_terms(a, c, middle)
        advance(c, middle)

    hats = hat_weight_table()
    slopes = lobatto_weights() / 2

    def hat_pair(lines):
        e1, e2 = lines[0] + lines[4], lines[1] + lines[3]
        whole_sum = mix(
            (hats[0, 0] + hats[0, 4], hats[0, 1] + hats[0, 3], hats[0, 2] * 2), (e1, e2, lines[2])
        )
        d1, d2 = lines[4] - lines[0], lines[3] - lines[1]
        gap = mix((hats[0, 0] - hats[0, 4], hats[0, 1] - hats[0, 3]), (d1, d2))
        return (0.5 * (whole_sum - gap), 0.5 * (whole_sum + gap))

    def plane(get):
        along = [hat_pair([get(p, q) for q in range(order)]) for p in range(order)]
        return [
            list(pair)
            for pair in zip(*[hat_pair([along[p][b] for p in range(order)]) for b in range(2)])
        ]

    parts = {}
    for a in range(3):

        def slope(p, q):
            f = [conv[(a,) + node(a, l, p, q)] for l in range(order)]
            return mix(slopes[:3], (f[0] + f[4], f[1] + f[3], f[2]))

        inside = plane(slope)
        bottom = plane(lambda p, q: conv[(a,) + node(a, 0, p, q)])
        open_end = jnp.where(jnp.logical_and(edges[a][0], me[a] == 0), 0.5, 0.0)
        for p in range(2):
            for q in range(2):
                for b in range(2):
                    key = node(a, b, p, q)
                    piece = inside[p][q] if b == 1 else open_end * bottom[p][q] - inside[p][q]
                    parts[key] = parts[key] + piece if key in parts else piece
    for a in (2, 1, 0):
        edge = edges[a][0]
        merged = {}
        for key in parts:
            if key[a] == 1:
                continue
            upper = key[:a] + (1,) + key[a + 1 :]
            moved = brick.move(parts[upper], a, True)
            if a == 1:
                moved = jnp.where(edge, roll(parts[upper], 1 - ey, 0), moved)
            merged[key] = parts[key] + jnp.where(edge, 0.0, moved)
            merged[upper] = jnp.where(edge, moved, 0.0)
        parts = merged
    for n, shift in enumerate(corners):
        send3[n] = parts[shift]
    each(round3, "start")
    each(round1x, "finish")
    each(round1, "finish")

    for a in range(3):
        for p in range(order):
            for q in range(order):
                out = lifted_derivative(
                    [conv[(a,) + node(a, l, p, q)] for l in range(order)], -1.0
                )
                for l in range(order):
                    where = node(a, l, p, q)
                    pres[where] = out[l] if a == 0 else pres[where] + out[l]

    eigen = eigen_value_table()
    slot_of = {}
    for key in itertools.combinations_with_replacement(range(order), 3):
        slot_of[key] = len(slot_of)
        size = float(np.prod([norm_squares[k] for k in key]))
        inverse[slot_of[key]] = 1.0 / (scale * float(sum(eigen[k] for k in key) / size) + 1.0 / size)

    for a in (0, 2, 1):
        each(pick(round2, a), "arrive")
        for s in range(2):
            own = order - 1 - face(s)
            for p in range(order):
                for q in range(order):
                    if a == 0:
                        far = far2_x[s, p, q]
                        far = far if s == 0 else roll(far, rows - ey, 0)
                    elif a == 1:
                        far = far2_y[s, p, q]
                    else:
                        far = unpack_entry(far2_z[s], p * order + q, s)
                    inside = brick.move(conv[(a,) + node(a, face(s), p, q)], a, s == 0)
                    side = half_lift * jnp.where(edges[a][s], far, inside)
                    where = node(a, own, p, q)
                    pres[where] = pres[where] + side if s == 0 else pres[where] - side

    def plane_modes(act, grid):
        grid = [act(grid[i]) for i in range(order)]
        cols = [act([grid[i][j] for i in range(order)]) for j in range(order)]
        return [[cols[j][i] for j in range(order)] for i in range(order)]

    span = range(order)
    for k in span:
        grid = plane_modes(to_modes, [[pres[i, j, k] for j in span] for i in span])
        for i in span:
            for j in span:
                pres[i, j, k] = grid[i][j]
    for batch in ((0, 1), (2, 3), (4,)):
        for i in batch:
            for j in span:
                modes = to_modes([pres[i, j, k] for k in span])
                modes = [modes[k] * inverse[slot_of[tuple(sorted((i, j, k)))]] for k in span]
                out = from_modes(modes)
                for k in span:
                    pres[i, j, k] = out[k]
        for k in span:
            index = ((lane + (ez - k)) * spread) % ez
            for i in batch:
                for j in span:
                    pres[i, j, k] = permute(pres[i, j, k], index)
    for i in span:
        for j in span:
            mixed = [None] * order
            for k in span:
                mixed[(turn * k) % order] = pres[i, j, k]
            natural = barrel(mixed, -1)
            for t in span:
                pres[i, j, t] = natural[t]
    for t in span:
        grid = plane_modes(from_modes, [[pres[i, j, t] for j in span] for i in span])
        for i in span:
            for j in span:
                for x in range(ex):
                    out_ref[i, t, pl.ds(x * pitch + j, ey, stride=order), :] = grid[i][j][
                        x * ey : (x + 1) * ey
                    ]

    each(round2, "finish")
    each(round3, "arrive")
    total = parts[(0, 0, 0)]
    for n in range(len(corners)):
        total = total + recv3[n]
    for x in range(ex):
        coarse_ref[x] = total[x * ey : (x + 1) * ey]
    each(round3, "finish")


def deliver(brick, packed_ref, part_ref, smooth_ref, coarse_ref, sems):
    ez, ny, pitch = brick.ez, brick.ny, brick.pitch
    copies = [pltpu.make_async_copy(part_ref, coarse_ref, sems.at[0])]
    for x in range(brick.ex):
        for t in range(order):
            copies.append(
                pltpu.make_async_copy(
                    packed_ref.at[:, t, x * pitch : x * pitch + ny],
                    smooth_ref.at[x * order : (x + 1) * order, :, t * ez : (t + 1) * ez],
                    sems.at[len(copies)],
                )
            )
    for copy in copies:
        copy.start()
    for copy in copies:
        copy.wait()


def shards(counts, velocity, mask, scale):
    ex, ey, ez = mask.shape
    brick = Brick(ex, ey, ez)
    tile = (brick.rows, ez)
    f32 = jnp.float32
    whole = pl.BlockSpec(memory_space=pltpu.VMEM)
    remote = pl.BlockSpec(memory_space=pltpu.HBM)
    sems = pltpu.SemaphoreType.DMA
    lines = (order, order)
    strips = (order, order, ex * brick.pitch, ez)
    triples = len(list(itertools.combinations_with_replacement(range(order), 3)))
    pairs = [(2,), (2,)]
    for n in (6, 2, 2, 2, 2, 2, len(corners)):
        pairs += [(n,), (n,)]

    def vmem(*shape):
        return pltpu.VMEM(shape, f32)

    packed, part = pl.pallas_call(
        functools.partial(body, brick, counts),
        out_shape=(
            jax.ShapeDtypeStruct(strips, f32),
            jax.ShapeDtypeStruct(mask.shape, f32),
        ),
        in_specs=[remote] * 3,
        out_specs=(whole, whole),
        scratch_shapes=[
            vmem(3, *strips),
            pltpu.VMEM(mask.shape, jnp.int32),
            vmem(*scale.shape),
            vmem(3, order, *lines, *tile),
            vmem(3, order, *lines, *tile),
            vmem(3, *strips[1:]),
            vmem(3, *lines, *tile),
            vmem(3, *lines, *tile),
            vmem(3, *lines, *tile),
            vmem(2, *tile),
            vmem(2, *tile),
            vmem(2, 3, *lines, *tile),
            vmem(3, 2, 2, *lines, *tile),
            vmem(order, *lines, *tile),
            vmem(triples, *tile),
            vmem(*lines, *tile),
            vmem(2, *lines, *tile),
            vmem(2, *lines, *tile),
            vmem(2, *tile),
            vmem(2, *tile),
            vmem(len(corners), *tile),
            vmem(len(corners), *tile),
        ]
        + [sems(shape) for shape in pairs],
        compiler_params=pltpu.CompilerParams(
            collective_id=0, has_side_effects=True, vmem_limit_bytes=32 << 20
        ),
    )(*[pltpu.with_memory_space_constraint(z, pltpu.HBM) for z in (velocity, mask, scale)])
    return pl.pallas_call(
        functools.partial(deliver, brick),
        out_shape=(
            jax.ShapeDtypeStruct(velocity.shape[1:], f32),
            jax.ShapeDtypeStruct(mask.shape, f32),
        ),
        in_specs=[whole] * 2,
        out_specs=(remote, remote),
        scratch_shapes=[sems((1 + ex * order,))],
        compiler_params=pltpu.CompilerParams(vmem_limit_bytes=16 << 20),
    )(packed, part)


def solution(mesh):
    counts = tuple(mesh.shape[name] for name in names)
    return jax.shard_map(
        functools.partial(shards, counts),
        mesh=mesh,
        in_specs=(P(None, "gx", "gy", "gz"), P("gx", "gy", "gz"), P("gx", "gy", "gz")),
        out_specs=(P("gx", "gy", "gz"), P("gx", "gy", "gz")),
        check_vma=False,
    )
```

```python
import functools
import itertools
import math

import jax
import jax.numpy as jnp
import numpy as np
from jax import lax
from jax.experimental import pallas as pl
from jax.experimental.pallas import tpu as pltpu
from jax.sharding import PartitionSpec as P

lift_factor = 10.0
time_step = 0.05
penalty = 4.0
half_lift = lift_factor * 0.5
order = 5
names = ("gx", "gy", "gz")
corners = [s for s in itertools.product((0, 1), repeat=3) if any(s)]
x_order = (0, 2, 1)


def lobatto_points():
    return np.array([-1.0, -math.sqrt(3.0 / 7.0), 0.0, math.sqrt(3.0 / 7.0), 1.0])


def lobatto_weights():
    return np.array([0.1, 49.0 / 90.0, 32.0 / 45.0, 49.0 / 90.0, 0.1])


def derivative_matrix():
    points = lobatto_points()
    scales = np.array(
        [np.prod([points[i] - points[k] for k in range(5) if k != i]) for i in range(5)]
    )
    result = np.zeros((5, 5))
    for i in range(5):
        for j in range(5):
            if i != j:
                result[i, j] = scales[i] / (scales[j] * (points[i] - points[j]))
        result[i, i] = -np.sum(result[i])
    return result


def eigen_value_table():
    return np.array([4.0 * math.sin(math.pi * k / 10.0) ** 2 for k in range(5)])


def hat_weight_table():
    points = lobatto_points()
    weights = lobatto_weights()
    return np.array([weights * (1.0 - points) / 2.0, weights * (1.0 + points) / 2.0])


def mix(coefs, terms):
    total = None
    for coef, term in zip(coefs, terms):
        if abs(coef) < 1e-12:
            continue
        piece = float(coef) * term
        total = piece if total is None else total + piece
    return total


def lifted_derivative(f, factor):
    d = derivative_matrix()
    d[0, 0] += half_lift
    d[4, 4] -= half_lift
    d = d * factor
    e1, e2 = f[0] + f[4], f[1] + f[3]
    o1, o2 = f[0] - f[4], f[1] - f[3]
    out = [None] * 5
    for i in range(2):
        even = mix(((d[i, 0] + d[i, 4]) / 2, (d[i, 1] + d[i, 3]) / 2, d[i, 2]), (e1, e2, f[2]))
        odd = mix(((d[i, 0] - d[i, 4]) / 2, (d[i, 1] - d[i, 3]) / 2), (o1, o2))
        out[i] = odd + even
        out[4 - i] = odd - even
    out[2] = mix((d[2, 0], d[2, 1]), (o1, o2))
    return out


cos18, cos54 = math.cos(math.pi * 0.1), math.cos(math.pi * 0.3)
cos36, cos72 = math.cos(math.pi * 0.2), math.cos(math.pi * 0.4)
even_gain = (cos36 + cos72) / 2
odd_ratio = cos54 / cos18
norm_squares = [0.2, 0.4 * cos18**2, 0.4, 0.4 * cos18**2, 0.4]


def to_modes(f):
    e1, e2 = f[0] + f[4], f[1] + f[3]
    o1, o2 = f[0] - f[4], f[1] - f[3]
    s = e1 + e2
    p = even_gain * (e1 - e2)
    q = 0.25 * s - f[2]
    return [s + f[2], o1 + odd_ratio * o2, p + q, odd_ratio * o1 - o2, p - q]


def from_modes(c):
    s, d = c[2] + c[4], c[2] - c[4]
    p = even_gain * s
    base = c[0] + 0.25 * d
    even = (base + p, base - p)
    odd = (c[1] + odd_ratio * c[3], odd_ratio * c[1] - c[3])
    return [even[0] + odd[0], even[1] + odd[1], c[0] - d, even[1] - odd[1], even[0] - odd[0]]


def roll(x, shift, axis):
    size = x.shape[axis]
    shift = shift % size
    return x if shift == 0 else pltpu.roll(x, shift, axis)


class Brick:
    def __init__(self, ex, ey, ez):
        self.ex, self.ey, self.ez = ex, ey, ez
        self.rows = ex * ey
        self.ny = ey * order
        self.pitch = -(-self.ny // 8) * 8

    def iotas(self):
        row = lax.broadcasted_iota(jnp.int32, (self.rows, self.ez), 0)
        lane = lax.broadcasted_iota(jnp.int32, (self.rows, self.ez), 1)
        return row, lane

    def slots(self, a):
        return (self.ex, self.ey, self.ez)[a]

    def place(self, a):
        row, lane = self.iotas()
        return (row // self.ey, row % self.ey, lane)[a]

    def move(self, x, a, up):
        step = (self.ey, 1, 1)[a]
        return roll(x, step if up else -step, x.ndim - (1 if a == 2 else 2))

    def edge(self, a, up):
        return self.place(a) == (0 if up else self.slots(a) - 1)


def body(
    brick,
    counts,
    v_ref,
    mask_ref,
    scale_ref,
    out_ref,
    coarse_ref,
    raw,
    mask_buf,
    scale_buf,
    vel,
    conv,
    strip_x,
    strip_e,
    far_zx,
    send2_y,
    raw_y,
    far_x,
    far_y,
    send_z,
    far_z,
    shifted,
    gain,
    pres,
    inverse,
    top2_x,
    far2_x,
    far2_y,
    send2_z,
    far2_z,
    send3,
    recv3,
    *sems,
):
    (load_sem, small_sem, se, re, szx, rzx, sx, rx, sy, ry, sz, rz, s2x, r2x, s2y, r2y, s2z, r2z, s3, r3) = sems
    ex, ey, ez, rows, ny, pitch = brick.ex, brick.ey, brick.ez, brick.rows, brick.ny, brick.pitch
    me = [lax.axis_index(name) for name in names]
    ends, middle = (0, order - 1), tuple(range(1, order - 1))

    def exists(shift):
        ok = None
        for a in range(3):
            if shift[a] > 0:
                one = me[a] < counts[a] - 1
            elif shift[a] < 0:
                one = me[a] > 0
            else:
                continue
            ok = one if ok is None else jnp.logical_and(ok, one)
        return ok

    def device(shift):
        return tuple(me[a] + shift[a] for a in range(3))

    unit = [tuple(int(a == b) for b in range(3)) for a in range(3)]

    def toward(a, s):
        return tuple((1 - 2 * s) * u for u in unit[a])

    partners = [toward(a, s) for a in range(3) for s in range(2)]
    greeted = partners + [(-1, -1, -1)]
    awaited = partners + [(1, 1, 1)]
    barrier = pltpu.get_barrier_semaphore()
    for shift in greeted:

        @pl.when(exists(shift))
        def _():
            pl.semaphore_signal(
                barrier, inc=1, device_id=device(shift), device_id_type=pl.DeviceIdType.MESH
            )

    for t in ends + middle:
        for x in range(ex):
            pltpu.make_async_copy(
                v_ref.at[:, x * order : (x + 1) * order, :, t * ez : (t + 1) * ez],
                raw.at[:, :, t, x * pitch : x * pitch + ny],
                load_sem.at[0 if t in ends else 1],
            ).start()
    small = [
        pltpu.make_async_copy(mask_ref, mask_buf, small_sem.at[0]),
        pltpu.make_async_copy(scale_ref, scale_buf, small_sem.at[1]),
    ]
    for copy in small:
        copy.start()

    def loaded(group):
        landed = raw.at[:, :, 0 : (2, order - 2)[group], 0 : ex * ny]
        pltpu.make_async_copy(landed, landed, load_sem.at[group]).wait()

    class Group:
        def __init__(self, shift, pairs, ssem, rsem, dst, whole=None):
            self.to, self.source = exists(shift), exists(tuple(-x for x in shift))
            self.dst = dst
            self.copies = [self.copy(src, to, ssem, rsem, shift) for src, to in pairs]
            self.all = self.copies[0] if whole is None else self.copy(whole, whole, ssem, rsem, shift)

        def copy(self, src, dst, ssem, rsem, shift):
            return pltpu.make_async_remote_copy(
                src_ref=src,
                dst_ref=dst,
                send_sem=ssem,
                recv_sem=rsem,
                device_id=device(shift),
                device_id_type=pl.DeviceIdType.MESH,
            )

        def start(self):
            @pl.when(self.to)
            def _():
                for copy in self.copies:
                    copy.start()

        def clear(self):
            @pl.when(jnp.logical_not(self.source))
            def _():
                self.dst[...] = jnp.zeros_like(self.dst)

        def arrive(self):
            @pl.when(self.source)
            def _():
                self.all.wait_recv()

        def finish(self):
            @pl.when(self.to)
            def _():
                self.all.wait_send()

    def y_rows(s):
        return [
            (x * ey + ey - 1, x * ey) if s == 0 else (x * ey, x * ey + ey - 1) for x in range(ex)
        ]

    def face(s):
        return order - 1 if s == 0 else 0

    round1x, round1e, round1, round2, round3 = {}, {}, {}, {}, {}
    for s in range(2):
        for c in range(3):
            n = c * 2 + s
            x, to = (ex - 1, 0) if s == 0 else (0, ex - 1)
            round1x[c, s] = Group(
                toward(0, s),
                [
                    (
                        raw.at[c, face(s), :, x * pitch : x * pitch + ny],
                        strip_x.at[c, :, to * pitch : to * pitch + ny],
                    )
                ],
                sx.at[n],
                rx.at[n],
                None,
            )
        round1e[0, s] = Group(
            toward(0, s),
            [
                (raw.at[0:2, face(s), :, x * pitch + r], strip_e.at[:, :, to * pitch + r])
                for r in (0, ny - 1)
            ],
            se.at[s],
            re.at[s],
            None,
            strip_e.at[:, :, 0:2],
        )
        round1e[1, s] = Group(
            toward(0, s), [(send_z, far_zx.at[s])], szx.at[s], rzx.at[s], None
        )
        line = ny - 1 if s == 0 else 0
        round1[1, s] = Group(
            toward(1, s),
            [
                (raw.at[:, :, :, x * pitch + line], raw_y.at[:, :, :, dst])
                for x, (_, dst) in enumerate(y_rows(s))
            ],
            sy.at[s],
            ry.at[s],
            None,
            raw_y.at[:, :, :, 0:ex],
        )
        round1[2, s] = Group(
            toward(2, s), [(send_z.at[s], far_z.at[s])], sz.at[s], rz.at[s], None
        )
        src = top2_x if s == 0 else conv.at[0, 0]
        round2[0, s] = Group(
            toward(0, s),
            [(src.at[:, :, 0:ey], far2_x.at[s, :, :, 0:ey])],
            s2x.at[s],
            r2x.at[s],
            far2_x.at[s],
        )
        round2[1, s] = Group(
            toward(1, s),
            [
                (send2_y.at[s, :, :, src], far2_y.at[s, :, :, dst])
                for src, dst in y_rows(s)
            ],
            s2y.at[s],
            r2y.at[s],
            far2_y.at[s],
            far2_y.at[s, :, :, 0:ex],
        )
        round2[2, s] = Group(
            toward(2, s), [(send2_z.at[s], far2_z.at[s])], s2z.at[s], r2z.at[s], far2_z.at[s]
        )
    for n, shift in enumerate(corners):
        round3[n] = Group(shift, [(send3.at[n], recv3.at[n])], s3.at[n], r3.at[n], recv3.at[n])

    def each(groups, act):
        for key in groups:
            getattr(groups[key], act)()

    def pick(groups, a):
        return {key: groups[key] for key in groups if key[0] == a}

    row, lane = brick.iotas()
    spread = pow(order, -1, ez)
    turn = pow(ez, -1, order)
    phase = (turn * lane) % order
    bits = [(phase & bit) != 0 for bit in (1, 2, 4)]
    place_x = brick.place(0)
    edges = [[brick.edge(a, s == 0) for s in range(2)] for a in range(3)]
    zero = jnp.zeros((rows, ez), jnp.float32)

    def known(a):
        here = [jnp.logical_and(edges[a][s], exists(toward(a, 1 - s))) for s in range(2)]
        return jnp.logical_or(*here)

    def permute(x, index):
        return jnp.take_along_axis(x, index, axis=1, mode="promise_in_bounds")

    def barrel(tiles, sign):
        for bit, on in zip((1, 2, 4), bits):
            tiles = [jnp.where(on, tiles[(m - sign * bit) % order], tiles[m]) for m in range(order)]
        return tiles

    def split_index(k):
        return (lane * order + k) % ez

    def pack_entry(total, tile, n, s):
        start = ez - 1 if s == 0 else 0
        return jnp.where(lane == n, roll(tile, n - start, 1), total)

    def unpack_entry(packed, n, s):
        return roll(packed, (0 if s == 0 else ez - 1) - n, 1)

    def fetch(strip, j):
        tile = None
        for x in range(ex):
            part = strip[pl.ds(j + x * (pitch - ny), rows, stride=order), :]
            tile = part if x == 0 else jnp.where(place_x == x, part, tile)
        return tile

    loaded(0)
    for s in range(2):
        packs = zero
        for n in range(3 * order * order):
            c, i, j = n // order**2, n // order % order, n % order
            packs = pack_entry(packs, fetch(raw.at[c, i, face(s)], j), n, s)
        send_z[s] = packs

    loaded(1)
    pl.semaphore_wait(barrier, sum(exists(shift).astype(jnp.int32) for shift in awaited))
    each(round1e, "start")
    each(round1, "start")
    for c in x_order:
        each(pick(round1x, c), "start")

    def gather(c, i):
        for j in range(order):
            merged = barrel([fetch(raw.at[c, i, t], j) for t in range(order)], 1)
            for k in range(order):
                vel[c, i, j, k] = merged[(turn * k) % order]

    def scatter(c, k):
        for i in range(order):
            for j in range(order):
                vel[c, i, j, k] = permute(vel[c, i, j, k], split_index(k))

    for i in range(order):
        gather(x_order[0], i)
    for n, c in enumerate(x_order):
        for k in range(order):
            scatter(c, k)
            if n < 2:
                gather(x_order[n + 1], k)

    each(round2, "clear")
    each(round3, "clear")

    def node(a, l, p, q):
        return ((l, p, q), (p, l, q), (p, q, l))[a]

    def lines(a, c, wanted):
        pairs = itertools.product(range(order), repeat=2)
        return [pq for pq in pairs if a == c or node(a, 0, *pq)[c] in wanted]

    def inner(c, wanted):
        for a in (c,) + tuple(b for b in range(3) if b != c):
            for p, q in lines(a, c, wanted):
                normal = [vel[(a,) + node(a, l, p, q)] for l in range(order)]
                moved = normal
                if a != c:
                    moved = [vel[(c,) + node(a, l, p, q)] for l in range(order)]
                out = lifted_derivative([n * w for n, w in zip(normal, moved)], -time_step)
                for l in wanted if a == c else range(order):
                    where = (c,) + node(a, l, p, q)
                    conv[where] = (moved[l] if a == c else conv[where]) + out[l]

    for c in x_order:
        inner(c, ends)
    for s in range(2):
        for c in range(3):
            for p in range(order):
                for q in range(order):
                    shifted[s, c, p, q] = brick.move(vel[c, p, q, face(s)], 2, s == 0)

    for copy in small:
        copy.wait()
    solid = jnp.concatenate([mask_buf[x] for x in range(ex)], axis=0).astype(jnp.float32)
    scale = jnp.concatenate([scale_buf[x] for x in range(ex)], axis=0)
    fluid = 1.0 / (1.0 + penalty * solid)

    def near(a, s, c, p, q):
        if a == 2:
            far = unpack_entry(far_z[s], (c * order + p) * order + q, s)
            far = jnp.where(exists(toward(2, 1 - s)), far, zero)
            return jnp.where(edges[2][s], far, shifted[s, c, p, q])
        far = far_x[c, p, q] if a == 0 else far_y[c, p, q]
        inside = brick.move(vel[(c,) + node(a, face(s), p, q)], a, s == 0)
        return jnp.where(edges[a][s], far, inside)

    step_lift = time_step * half_lift

    def face_terms(a, c, wanted):
        for s in range(2):
            own = order - 1 - face(s)
            for p, q in lines(a, c, wanted):
                where = (c,) + node(a, own, p, q)
                moved, moved_out = vel[where], near(a, s, c, p, q)
                if a == c:
                    down = step_lift * jnp.maximum(jnp.abs(moved), jnp.abs(moved_out))
                    flow = step_lift * moved_out
                    across = down + flow if s == 0 else down - flow
                    gain[a, s, 0, p, q] = across
                    gain[a, s, 1, p, q] = down
                else:
                    across, down = gain[a, s, 0, p, q], gain[a, s, 1, p, q]
                conv[where] = conv[where] + (across * moved_out - down * moved)

    def advance(c, wanted):
        for l in wanted:
            for p in range(order):
                for q in range(order):
                    where = (c,) + node(c, l, p, q)
                    conv[where] = conv[where] * fluid

    each(round1, "arrive")
    each(round1e, "arrive")
    for c in (2, 0, 1):
        face_terms(2, c, ends)

    valid = known(1)
    for i in range(order):
        mixed = {}
        for c in range(3):
            mixed[c] = barrel([jnp.where(valid, raw_y[c, i, t], zero) for t in range(order)], 1)
        for k in range(order):
            for c in range(3):
                far_y[c, i, k] = permute(mixed[c][(turn * k) % order], split_index(k))
    for c in (1, 0, 2):
        face_terms(1, c, ends)

    valid_x = known(0)

    def split_x(strip, todo):
        mixed = {}
        for j in todo:
            natural = [jnp.where(valid_x, fetch(strip.at[t], j), zero) for t in range(order)]
            mixed[j] = barrel(natural, 1)
        return {
            (j, k): permute(mixed[j][(turn * k) % order], split_index(k))
            for k in range(order)
            for j in todo
        }

    def edge_value(c, s, j, k, far_normal, far_moved):
        own = order - 1 - face(s)

        def outside(b, far):
            return jnp.where(edges[0][s], far, brick.move(vel[b, face(s), j, k], 0, s == 0))

        normal, normal_out = vel[0, own, j, k], outside(0, far_normal)
        down = step_lift * jnp.maximum(jnp.abs(normal), jnp.abs(normal_out))
        flow = step_lift * normal_out
        across = down + flow if s == 0 else down - flow
        term = across * outside(c, far_moved) - down * vel[c, own, j, k]
        return (conv[c, own, j, k] + term) * fluid

    packed_ends = []
    for s in range(2):
        low = roll(far_zx[0, s], -(ex - 1) * ey, 0)
        high = roll(roll(far_zx[1, s], (ex - 1) * ey, 0), (order - 1) * order, 1)
        packed_ends.append(jnp.where(valid_x, jnp.where(place_x == 0, low, high), zero))

    def far_end(c, j, s):
        n = (c * order + order - 1) * order + j
        return roll(packed_ends[s], (ez - 1 if s == 0 else 0) - n, 1)

    far_e = [split_x(strip_e.at[c], ends) for c in range(2)]
    for s in range(2):
        packs = zero
        for j in range(order):
            far_pair = far_end(0, j, s), far_end(2, j, s)
            for i in range(order):
                if i in ends:
                    side = 0 if i == 0 else 1
                    tile = edge_value(2, side, j, face(s), *far_pair)
                else:
                    tile = conv[2, i, j, face(s)] * fluid
                packs = pack_entry(packs, tile, i * order + j, s)
        send2_z[s] = packs
    for s in range(2):
        for k in range(order):
            far_pair = far_e[0][face(s), k], far_e[1][face(s), k]
            for i in range(order):
                if i in ends:
                    side = 0 if i == 0 else 1
                    send2_y[s, i, k] = edge_value(1, side, face(s), k, *far_pair)
                else:
                    send2_y[s, i, k] = conv[1, i, face(s), k] * fluid
    each(pick(round2, 2), "start")
    each(pick(round2, 1), "start")

    def whole_x(c):
        each(pick(round1x, c), "arrive")
        far = split_x(strip_x.at[c], range(order))
        for j, k in far:
            far_x[c, j, k] = far[j, k]

    whole_x(0)
    face_terms(0, 0, ends)
    advance(0, ends)
    for j in range(order):
        for k in range(order):
            top2_x[j, k] = roll(conv[0, order - 1, j, k], ey - rows, 0)
    each(pick(round2, 0), "start")

    for c in range(3):
        inner(c, middle)
        for a in (1, 2):
            if a != c:
                face_terms(a, c, middle)
    advance(0, middle)
    for c in x_order[1:]:
        whole_x(c)
        face_terms(0, c, range(order))
        advance(c, range(order))

    hats = hat_weight_table()
    slopes = lobatto_weights() / 2

    def hat_pair(lines):
        e1, e2 = lines[0] + lines[4], lines[1] + lines[3]
        whole_sum = mix(
            (hats[0, 0] + hats[0, 4], hats[0, 1] + hats[0, 3], hats[0, 2] * 2), (e1, e2, lines[2])
        )
        d1, d2 = lines[4] - lines[0], lines[3] - lines[1]
        gap = mix((hats[0, 0] - hats[0, 4], hats[0, 1] - hats[0, 3]), (d1, d2))
        return (0.5 * (whole_sum - gap), 0.5 * (whole_sum + gap))

    def plane(get):
        along = [hat_pair([get(p, q) for q in range(order)]) for p in range(order)]
        return [
            list(pair)
            for pair in zip(*[hat_pair([along[p][b] for p in range(order)]) for b in range(2)])
        ]

    parts = {}
    for a in range(3):

        def slope(p, q):
            f = [conv[(a,) + node(a, l, p, q)] for l in range(order)]
            return mix(slopes[:3], (f[0] + f[4], f[1] + f[3], f[2]))

        inside = plane(slope)
        bottom = plane(lambda p, q: conv[(a,) + node(a, 0, p, q)])
        open_end = jnp.where(jnp.logical_and(edges[a][0], me[a] == 0), 0.5, 0.0)
        for p in range(2):
            for q in range(2):
                for b in range(2):
                    key = node(a, b, p, q)
                    piece = inside[p][q] if b == 1 else open_end * bottom[p][q] - inside[p][q]
                    parts[key] = parts[key] + piece if key in parts else piece
    for a in (2, 1, 0):
        edge = edges[a][0]
        merged = {}
        for key in parts:
            if key[a] == 1:
                continue
            upper = key[:a] + (1,) + key[a + 1 :]
            moved = brick.move(parts[upper], a, True)
            if a == 1:
                moved = jnp.where(edge, roll(parts[upper], 1 - ey, 0), moved)
            merged[key] = parts[key] + jnp.where(edge, 0.0, moved)
            merged[upper] = jnp.where(edge, moved, 0.0)
        parts = merged
    for n, shift in enumerate(corners):
        send3[n] = parts[shift]
    each(round3, "start")
    each(round1x, "finish")
    each(round1e, "finish")
    each(round1, "finish")

    for a in range(3):
        for p in range(order):
            for q in range(order):
                out = lifted_derivative(
                    [conv[(a,) + node(a, l, p, q)] for l in range(order)], -1.0
                )
                for l in range(order):
                    where = node(a, l, p, q)
                    pres[where] = out[l] if a == 0 else pres[where] + out[l]

    eigen = eigen_value_table()
    slot_of = {}
    for key in itertools.combinations_with_replacement(range(order), 3):
        slot_of[key] = len(slot_of)
        size = float(np.prod([norm_squares[k] for k in key]))
        inverse[slot_of[key]] = 1.0 / (scale * float(sum(eigen[k] for k in key) / size) + 1.0 / size)

    def far_faces(a):
        each(pick(round2, a), "arrive")
        for s in range(2):
            own = order - 1 - face(s)
            for p in range(order):
                for q in range(order):
                    if a == 0:
                        far = far2_x[s, p, q]
                        far = far if s == 0 else roll(far, rows - ey, 0)
                    elif a == 1:
                        far = far2_y[s, p, q]
                    else:
                        far = unpack_entry(far2_z[s], p * order + q, s)
                    inside = brick.move(conv[(a,) + node(a, face(s), p, q)], a, s == 0)
                    side = half_lift * jnp.where(edges[a][s], far, inside)
                    where = node(a, own, p, q)
                    pres[where] = pres[where] + side if s == 0 else pres[where] - side

    span = range(order)

    def layer_modes(i):
        grid = [to_modes([pres[i, j, k] for k in span]) for j in span]
        cols = [to_modes([grid[j][k] for j in span]) for k in span]
        for j in span:
            for k in span:
                pres[i, j, k] = cols[k][j]

    far_faces(2)
    far_faces(1)
    for i in middle:
        layer_modes(i)
    far_faces(0)
    for i in ends:
        layer_modes(i)
    for j in span:
        for k in span:
            modes = to_modes([pres[i, j, k] for i in span])
            modes = [modes[i] * inverse[slot_of[tuple(sorted((i, j, k)))]] for i in span]
            out = from_modes(modes)
            for i in span:
                pres[i, j, k] = out[i]

    def turned(batch):
        for i in batch:
            for j in span:
                out = from_modes([pres[i, j, k] for k in span])
                for k in span:
                    pres[i, j, k] = out[k]
        for k in span:
            index = ((lane + (ez - k)) * spread) % ez
            for i in batch:
                for j in span:
                    pres[i, j, k] = permute(pres[i, j, k], index)

    def written(batch):
        for i in batch:
            for j in span:
                mixed = [None] * order
                for k in span:
                    mixed[(turn * k) % order] = pres[i, j, k]
                natural = barrel(mixed, -1)
                for t in span:
                    pres[i, j, t] = natural[t]
            for t in span:
                out = from_modes([pres[i, j, t] for j in span])
                for j in span:
                    for x in range(ex):
                        out_ref[i, t, pl.ds(x * pitch + j, ey, stride=order), :] = out[j][
                            x * ey : (x + 1) * ey
                        ]

    batches = ((0, 1), (2, 3), (4,))
    turned(batches[0])
    for n in range(1, len(batches)):
        turned(batches[n])
        written(batches[n - 1])
    written(batches[-1])

    each(round2, "finish")
    each(round3, "arrive")
    total = parts[(0, 0, 0)]
    for n in range(len(corners)):
        total = total + recv3[n]
    for x in range(ex):
        coarse_ref[x] = total[x * ey : (x + 1) * ey]
    each(round3, "finish")


def deliver(brick, packed_ref, part_ref, smooth_ref, coarse_ref, sems):
    ez, ny, pitch = brick.ez, brick.ny, brick.pitch
    copies = [pltpu.make_async_copy(part_ref, coarse_ref, sems.at[0])]
    for x in range(brick.ex):
        for t in range(order):
            copies.append(
                pltpu.make_async_copy(
                    packed_ref.at[:, t, x * pitch : x * pitch + ny],
                    smooth_ref.at[x * order : (x + 1) * order, :, t * ez : (t + 1) * ez],
                    sems.at[len(copies)],
                )
            )
    for copy in copies:
        copy.start()
    for copy in copies:
        copy.wait()


def shards(counts, velocity, mask, scale):
    ex, ey, ez = mask.shape
    brick = Brick(ex, ey, ez)
    tile = (brick.rows, ez)
    f32 = jnp.float32
    whole = pl.BlockSpec(memory_space=pltpu.VMEM)
    remote = pl.BlockSpec(memory_space=pltpu.HBM)
    sems = pltpu.SemaphoreType.DMA
    lines = (order, order)
    strips = (order, order, ex * brick.pitch, ez)
    triples = len(list(itertools.combinations_with_replacement(range(order), 3)))
    pairs = [(2,), (2,)]
    for n in (2, 2, 6, 2, 2, 2, 2, 2, len(corners)):
        pairs += [(n,), (n,)]

    def vmem(*shape):
        return pltpu.VMEM(shape, f32)

    packed, part = pl.pallas_call(
        functools.partial(body, brick, counts),
        out_shape=(
            jax.ShapeDtypeStruct(strips, f32),
            jax.ShapeDtypeStruct(mask.shape, f32),
        ),
        in_specs=[remote] * 3,
        out_specs=(whole, whole),
        scratch_shapes=[
            vmem(3, *strips),
            pltpu.VMEM(mask.shape, jnp.int32),
            vmem(*scale.shape),
            vmem(3, order, *lines, *tile),
            vmem(3, order, *lines, *tile),
            vmem(3, *strips[1:]),
            vmem(2, *strips[1:]),
            vmem(2, 2, *tile),
            vmem(2, *lines, *tile),
            vmem(3, *lines, *tile),
            vmem(3, *lines, *tile),
            vmem(3, *lines, *tile),
            vmem(2, *tile),
            vmem(2, *tile),
            vmem(2, 3, *lines, *tile),
            vmem(3, 2, 2, *lines, *tile),
            vmem(order, *lines, *tile),
            vmem(triples, *tile),
            vmem(*lines, *tile),
            vmem(2, *lines, *tile),
            vmem(2, *lines, *tile),
            vmem(2, *tile),
            vmem(2, *tile),
            vmem(len(corners), *tile),
            vmem(len(corners), *tile),
        ]
        + [sems(shape) for shape in pairs],
        compiler_params=pltpu.CompilerParams(
            collective_id=0, has_side_effects=True, vmem_limit_bytes=32 << 20
        ),
    )(*[pltpu.with_memory_space_constraint(z, pltpu.HBM) for z in (velocity, mask, scale)])
    return pl.pallas_call(
        functools.partial(deliver, brick),
        out_shape=(
            jax.ShapeDtypeStruct(velocity.shape[1:], f32),
            jax.ShapeDtypeStruct(mask.shape, f32),
        ),
        in_specs=[whole] * 2,
        out_specs=(remote, remote),
        scratch_shapes=[sems((1 + ex * order,))],
        compiler_params=pltpu.CompilerParams(vmem_limit_bytes=16 << 20),
    )(packed, part)


def solution(mesh):
    counts = tuple(mesh.shape[name] for name in names)
    return jax.shard_map(
        functools.partial(shards, counts),
        mesh=mesh,
        in_specs=(P(None, "gx", "gy", "gz"), P("gx", "gy", "gz"), P("gx", "gy", "gz")),
        out_specs=(P("gx", "gy", "gz"), P("gx", "gy", "gz")),
        check_vma=False,
    )
```

```python
import functools
import itertools
import math

import jax
import jax.numpy as jnp
import numpy as np
from jax import lax
from jax.experimental import pallas as pl
from jax.experimental.pallas import tpu as pltpu
from jax.sharding import PartitionSpec as P

lift_factor = 10.0
time_step = 0.05
penalty = 4.0
half_lift = lift_factor * 0.5
order = 5
names = ("gx", "gy", "gz")
corners = [s for s in itertools.product((0, 1), repeat=3) if any(s)]
x_order = (0, 2, 1)


def lobatto_points():
    return np.array([-1.0, -math.sqrt(3.0 / 7.0), 0.0, math.sqrt(3.0 / 7.0), 1.0])


def lobatto_weights():
    return np.array([0.1, 49.0 / 90.0, 32.0 / 45.0, 49.0 / 90.0, 0.1])


def derivative_matrix():
    points = lobatto_points()
    scales = np.array(
        [np.prod([points[i] - points[k] for k in range(5) if k != i]) for i in range(5)]
    )
    result = np.zeros((5, 5))
    for i in range(5):
        for j in range(5):
            if i != j:
                result[i, j] = scales[i] / (scales[j] * (points[i] - points[j]))
        result[i, i] = -np.sum(result[i])
    return result


def eigen_value_table():
    return np.array([4.0 * math.sin(math.pi * k / 10.0) ** 2 for k in range(5)])


def hat_weight_table():
    points = lobatto_points()
    weights = lobatto_weights()
    return np.array([weights * (1.0 - points) / 2.0, weights * (1.0 + points) / 2.0])


def mix(coefs, terms):
    total = None
    for coef, term in zip(coefs, terms):
        if abs(coef) < 1e-12:
            continue
        piece = float(coef) * term
        total = piece if total is None else total + piece
    return total


def lifted_derivative(f, factor):
    d = derivative_matrix()
    d[0, 0] += half_lift
    d[4, 4] -= half_lift
    d = d * factor
    e1, e2 = f[0] + f[4], f[1] + f[3]
    o1, o2 = f[0] - f[4], f[1] - f[3]
    out = [None] * 5
    for i in range(2):
        even = mix(((d[i, 0] + d[i, 4]) / 2, (d[i, 1] + d[i, 3]) / 2, d[i, 2]), (e1, e2, f[2]))
        odd = mix(((d[i, 0] - d[i, 4]) / 2, (d[i, 1] - d[i, 3]) / 2), (o1, o2))
        out[i] = odd + even
        out[4 - i] = odd - even
    out[2] = mix((d[2, 0], d[2, 1]), (o1, o2))
    return out


cos18, cos54 = math.cos(math.pi * 0.1), math.cos(math.pi * 0.3)
cos36, cos72 = math.cos(math.pi * 0.2), math.cos(math.pi * 0.4)
even_gain = (cos36 + cos72) / 2
odd_ratio = cos54 / cos18
norm_squares = [0.2, 0.4 * cos18**2, 0.4, 0.4 * cos18**2, 0.4]


def to_modes(f):
    e1, e2 = f[0] + f[4], f[1] + f[3]
    o1, o2 = f[0] - f[4], f[1] - f[3]
    s = e1 + e2
    p = even_gain * (e1 - e2)
    q = 0.25 * s - f[2]
    return [s + f[2], o1 + odd_ratio * o2, p + q, odd_ratio * o1 - o2, p - q]


def from_modes(c):
    s, d = c[2] + c[4], c[2] - c[4]
    p = even_gain * s
    base = c[0] + 0.25 * d
    even = (base + p, base - p)
    odd = (c[1] + odd_ratio * c[3], odd_ratio * c[1] - c[3])
    return [even[0] + odd[0], even[1] + odd[1], c[0] - d, even[1] - odd[1], even[0] - odd[0]]


def roll(x, shift, axis):
    size = x.shape[axis]
    shift = shift % size
    return x if shift == 0 else pltpu.roll(x, shift, axis)


class Brick:
    def __init__(self, ex, ey, ez):
        self.ex, self.ey, self.ez = ex, ey, ez
        self.rows = ex * ey
        self.ny = ey * order
        self.pitch = -(-self.ny // 8) * 8

    def iotas(self):
        row = lax.broadcasted_iota(jnp.int32, (self.rows, self.ez), 0)
        lane = lax.broadcasted_iota(jnp.int32, (self.rows, self.ez), 1)
        return row, lane

    def slots(self, a):
        return (self.ex, self.ey, self.ez)[a]

    def place(self, a):
        row, lane = self.iotas()
        return (row // self.ey, row % self.ey, lane)[a]

    def move(self, x, a, up):
        step = (self.ey, 1, 1)[a]
        return roll(x, step if up else -step, x.ndim - (1 if a == 2 else 2))

    def edge(self, a, up):
        return self.place(a) == (0 if up else self.slots(a) - 1)


def body(
    brick,
    counts,
    v_ref,
    mask_ref,
    scale_ref,
    out_ref,
    coarse_ref,
    raw,
    mask_buf,
    scale_buf,
    vel,
    conv,
    strip_x,
    strip_e,
    far_zx,
    send2_y,
    raw_y,
    far_x,
    far_y,
    send_z,
    far_z,
    shifted,
    gain,
    pres,
    inverse,
    top2_x,
    far2_x,
    far2_y,
    send2_z,
    far2_z,
    send3,
    recv3,
    *sems,
):
    (load_sem, small_sem, se, re, szx, rzx, sx, rx, sy, ry, sz, rz, s2x, r2x, s2y, r2y, s2z, r2z, s3, r3) = sems
    ex, ey, ez, rows, ny, pitch = brick.ex, brick.ey, brick.ez, brick.rows, brick.ny, brick.pitch
    me = [lax.axis_index(name) for name in names]
    ends, middle = (0, order - 1), tuple(range(1, order - 1))

    def exists(shift):
        ok = None
        for a in range(3):
            if shift[a] > 0:
                one = me[a] < counts[a] - 1
            elif shift[a] < 0:
                one = me[a] > 0
            else:
                continue
            ok = one if ok is None else jnp.logical_and(ok, one)
        return ok

    def device(shift):
        return tuple(me[a] + shift[a] for a in range(3))

    unit = [tuple(int(a == b) for b in range(3)) for a in range(3)]

    def toward(a, s):
        return tuple((1 - 2 * s) * u for u in unit[a])

    partners = [toward(a, s) for a in range(3) for s in range(2)]
    greeted = partners + [(-1, -1, -1)]
    awaited = partners + [(1, 1, 1)]
    barrier = pltpu.get_barrier_semaphore()
    for shift in greeted:

        @pl.when(exists(shift))
        def _():
            pl.semaphore_signal(
                barrier, inc=1, device_id=device(shift), device_id_type=pl.DeviceIdType.MESH
            )

    for t in ends + middle:
        for x in range(ex):
            pltpu.make_async_copy(
                v_ref.at[:, x * order : (x + 1) * order, :, t * ez : (t + 1) * ez],
                raw.at[:, :, t, x * pitch : x * pitch + ny],
                load_sem.at[0 if t in ends else 1],
            ).start()
    small = [
        pltpu.make_async_copy(mask_ref, mask_buf, small_sem.at[0]),
        pltpu.make_async_copy(scale_ref, scale_buf, small_sem.at[1]),
    ]
    for copy in small:
        copy.start()

    def loaded(group):
        landed = raw.at[:, :, 0 : (2, order - 2)[group], 0 : ex * ny]
        pltpu.make_async_copy(landed, landed, load_sem.at[group]).wait()

    class Group:
        def __init__(self, shift, pairs, ssem, rsem, dst, whole=None):
            self.to, self.source = exists(shift), exists(tuple(-x for x in shift))
            self.dst = dst
            self.copies = [self.copy(src, to, ssem, rsem, shift) for src, to in pairs]
            self.all = self.copies[0] if whole is None else self.copy(whole, whole, ssem, rsem, shift)

        def copy(self, src, dst, ssem, rsem, shift):
            return pltpu.make_async_remote_copy(
                src_ref=src,
                dst_ref=dst,
                send_sem=ssem,
                recv_sem=rsem,
                device_id=device(shift),
                device_id_type=pl.DeviceIdType.MESH,
            )

        def start(self):
            @pl.when(self.to)
            def _():
                for copy in self.copies:
                    copy.start()

        def clear(self):
            @pl.when(jnp.logical_not(self.source))
            def _():
                self.dst[...] = jnp.zeros_like(self.dst)

        def arrive(self):
            @pl.when(self.source)
            def _():
                self.all.wait_recv()

        def finish(self):
            @pl.when(self.to)
            def _():
                self.all.wait_send()

    def y_rows(s):
        return [
            (x * ey + ey - 1, x * ey) if s == 0 else (x * ey, x * ey + ey - 1) for x in range(ex)
        ]

    def face(s):
        return order - 1 if s == 0 else 0

    round1x, round1e, round1, round2, round3 = {}, {}, {}, {}, {}
    for s in range(2):
        for c in range(3):
            n = c * 2 + s
            x, to = (ex - 1, 0) if s == 0 else (0, ex - 1)
            round1x[c, s] = Group(
                toward(0, s),
                [
                    (
                        raw.at[c, face(s), :, x * pitch : x * pitch + ny],
                        strip_x.at[c, :, to * pitch : to * pitch + ny],
                    )
                ],
                sx.at[n],
                rx.at[n],
                None,
            )
        round1e[0, s] = Group(
            toward(0, s),
            [
                (raw.at[0:2, face(s), :, x * pitch + r], strip_e.at[:, :, to * pitch + r])
                for r in (0, ny - 1)
            ],
            se.at[s],
            re.at[s],
            None,
            strip_e.at[:, :, 0:2],
        )
        round1e[1, s] = Group(
            toward(0, s), [(send_z, far_zx.at[s])], szx.at[s], rzx.at[s], None
        )
        line = ny - 1 if s == 0 else 0
        round1[1, s] = Group(
            toward(1, s),
            [
                (raw.at[:, :, :, x * pitch + line], raw_y.at[:, :, :, dst])
                for x, (_, dst) in enumerate(y_rows(s))
            ],
            sy.at[s],
            ry.at[s],
            None,
            raw_y.at[:, :, :, 0:ex],
        )
        round1[2, s] = Group(
            toward(2, s), [(send_z.at[s], far_z.at[s])], sz.at[s], rz.at[s], None
        )
        src = top2_x if s == 0 else conv.at[0, 0]
        round2[0, s] = Group(
            toward(0, s),
            [(src.at[:, :, 0:ey], far2_x.at[s, :, :, 0:ey])],
            s2x.at[s],
            r2x.at[s],
            far2_x.at[s],
        )
        round2[1, s] = Group(
            toward(1, s),
            [
                (send2_y.at[s, :, :, src], far2_y.at[s, :, :, dst])
                for src, dst in y_rows(s)
            ],
            s2y.at[s],
            r2y.at[s],
            far2_y.at[s],
            far2_y.at[s, :, :, 0:ex],
        )
        round2[2, s] = Group(
            toward(2, s), [(send2_z.at[s], far2_z.at[s])], s2z.at[s], r2z.at[s], far2_z.at[s]
        )
    for n, shift in enumerate(corners):
        round3[n] = Group(shift, [(send3.at[n], recv3.at[n])], s3.at[n], r3.at[n], recv3.at[n])

    def each(groups, act):
        for key in groups:
            getattr(groups[key], act)()

    def pick(groups, a):
        return {key: groups[key] for key in groups if key[0] == a}

    row, lane = brick.iotas()
    spread = pow(order, -1, ez)
    turn = pow(ez, -1, order)
    phase = (turn * lane) % order
    bits = [(phase & bit) != 0 for bit in (1, 2, 4)]
    place_x = brick.place(0)
    edges = [[brick.edge(a, s == 0) for s in range(2)] for a in range(3)]
    zero = jnp.zeros((rows, ez), jnp.float32)

    def known(a):
        here = [jnp.logical_and(edges[a][s], exists(toward(a, 1 - s))) for s in range(2)]
        return jnp.logical_or(*here)

    def permute(x, index):
        return jnp.take_along_axis(x, index, axis=1, mode="promise_in_bounds")

    def barrel(tiles, sign):
        for bit, on in zip((1, 2, 4), bits):
            tiles = [jnp.where(on, tiles[(m - sign * bit) % order], tiles[m]) for m in range(order)]
        return tiles

    def split_index(k):
        return (lane * order + k) % ez

    def pack_entry(total, tile, n, s):
        start = ez - 1 if s == 0 else 0
        return jnp.where(lane == n, roll(tile, n - start, 1), total)

    def unpack_entry(packed, n, s):
        return roll(packed, (0 if s == 0 else ez - 1) - n, 1)

    def fetch(strip, j):
        tile = None
        for x in range(ex):
            part = strip[pl.ds(j + x * (pitch - ny), rows, stride=order), :]
            tile = part if x == 0 else jnp.where(place_x == x, part, tile)
        return tile

    loaded(0)
    for s in range(2):
        packs = zero
        for n in range(3 * order * order):
            c, i, j = n // order**2, n // order % order, n % order
            packs = pack_entry(packs, fetch(raw.at[c, i, face(s)], j), n, s)
        send_z[s] = packs

    loaded(1)
    pl.semaphore_wait(barrier, sum(exists(shift).astype(jnp.int32) for shift in awaited))
    each(round1e, "start")
    each(round1, "start")
    for c in x_order:
        each(pick(round1x, c), "start")

    def gather(c, i):
        for j in range(order):
            merged = barrel([fetch(raw.at[c, i, t], j) for t in range(order)], 1)
            for k in range(order):
                vel[c, i, j, k] = merged[(turn * k) % order]

    def scatter(c, k):
        for i in range(order):
            for j in range(order):
                vel[c, i, j, k] = permute(vel[c, i, j, k], split_index(k))

    for i in range(order):
        gather(x_order[0], i)
    for n, c in enumerate(x_order):
        for k in range(order):
            scatter(c, k)
            if n < 2:
                gather(x_order[n + 1], k)

    each(round2, "clear")
    each(round3, "clear")

    def node(a, l, p, q):
        return ((l, p, q), (p, l, q), (p, q, l))[a]

    def lines(a, c, wanted):
        pairs = itertools.product(range(order), repeat=2)
        return [pq for pq in pairs if a == c or node(a, 0, *pq)[c] in wanted]

    def inner(c, wanted):
        for a in (c,) + tuple(b for b in range(3) if b != c):
            for p, q in lines(a, c, wanted):
                normal = [vel[(a,) + node(a, l, p, q)] for l in range(order)]
                moved = normal
                if a != c:
                    moved = [vel[(c,) + node(a, l, p, q)] for l in range(order)]
                out = lifted_derivative([n * w for n, w in zip(normal, moved)], -time_step)
                for l in wanted if a == c else range(order):
                    where = (c,) + node(a, l, p, q)
                    conv[where] = (moved[l] if a == c else conv[where]) + out[l]

    for c in x_order:
        inner(c, ends)
    for s in range(2):
        for c in range(3):
            for p in range(order):
                for q in range(order):
                    shifted[s, c, p, q] = brick.move(vel[c, p, q, face(s)], 2, s == 0)

    for copy in small:
        copy.wait()
    solid = jnp.concatenate([mask_buf[x] for x in range(ex)], axis=0).astype(jnp.float32)
    scale = jnp.concatenate([scale_buf[x] for x in range(ex)], axis=0)
    fluid = 1.0 / (1.0 + penalty * solid)

    def near(a, s, c, p, q):
        if a == 2:
            far = unpack_entry(far_z[s], (c * order + p) * order + q, s)
            far = jnp.where(exists(toward(2, 1 - s)), far, zero)
            return jnp.where(edges[2][s], far, shifted[s, c, p, q])
        far = far_x[c, p, q] if a == 0 else far_y[c, p, q]
        inside = brick.move(vel[(c,) + node(a, face(s), p, q)], a, s == 0)
        return jnp.where(edges[a][s], far, inside)

    step_lift = time_step * half_lift

    def face_terms(a, c, wanted):
        for s in range(2):
            own = order - 1 - face(s)
            for p, q in lines(a, c, wanted):
                where = (c,) + node(a, own, p, q)
                moved, moved_out = vel[where], near(a, s, c, p, q)
                if a == c:
                    down = step_lift * jnp.maximum(jnp.abs(moved), jnp.abs(moved_out))
                    flow = step_lift * moved_out
                    across = down + flow if s == 0 else down - flow
                    gain[a, s, 0, p, q] = across
                    gain[a, s, 1, p, q] = down
                else:
                    across, down = gain[a, s, 0, p, q], gain[a, s, 1, p, q]
                conv[where] = conv[where] + (across * moved_out - down * moved)

    def advance(c, wanted):
        for l in wanted:
            for p in range(order):
                for q in range(order):
                    where = (c,) + node(c, l, p, q)
                    conv[where] = conv[where] * fluid

    each(round1, "arrive")
    each(round1e, "arrive")
    valid = known(1)

    def merge_y(c, todo):
        for i in todo:
            mixed = barrel([jnp.where(valid, raw_y[c, i, t], zero) for t in range(order)], 1)
            for k in range(order):
                far_y[c, i, k] = mixed[(turn * k) % order]

    def turn_y(c, todo, planes):
        for k in planes:
            for i in todo:
                far_y[c, i, k] = permute(far_y[c, i, k], split_index(k))

    whole = range(order)
    merge_y(1, whole)
    merge_y(0, ends)
    merge_y(2, whole)
    for k in whole:
        turn_y(1, whole, (k,))
        turn_y(0, ends, (k,))
        if k in ends:
            turn_y(2, whole, (k,))
    face_terms(2, 2, ends)
    face_terms(2, 0, ends)
    face_terms(1, 1, ends)
    face_terms(1, 2, ends)
    face_terms(1, 0, ends)

    valid_x = known(0)

    def split_x(strip, todo):
        mixed = {}
        for j in todo:
            natural = [jnp.where(valid_x, fetch(strip.at[t], j), zero) for t in range(order)]
            mixed[j] = barrel(natural, 1)
        return {
            (j, k): permute(mixed[j][(turn * k) % order], split_index(k))
            for k in range(order)
            for j in todo
        }

    def edge_value(c, s, j, k, far_normal, far_moved):
        own = order - 1 - face(s)

        def outside(b, far):
            return jnp.where(edges[0][s], far, brick.move(vel[b, face(s), j, k], 0, s == 0))

        normal, normal_out = vel[0, own, j, k], outside(0, far_normal)
        down = step_lift * jnp.maximum(jnp.abs(normal), jnp.abs(normal_out))
        flow = step_lift * normal_out
        across = down + flow if s == 0 else down - flow
        term = across * outside(c, far_moved) - down * vel[c, own, j, k]
        return (conv[c, own, j, k] + term) * fluid

    packed_ends = []
    for s in range(2):
        low = roll(far_zx[0, s], -(ex - 1) * ey, 0)
        high = roll(roll(far_zx[1, s], (ex - 1) * ey, 0), (order - 1) * order, 1)
        packed_ends.append(jnp.where(valid_x, jnp.where(place_x == 0, low, high), zero))

    def far_end(c, j, s):
        n = (c * order + order - 1) * order + j
        return roll(packed_ends[s], (ez - 1 if s == 0 else 0) - n, 1)

    for s in range(2):
        packs = zero
        for j in range(order):
            far_pair = far_end(0, j, s), far_end(2, j, s)
            for i in range(order):
                if i in ends:
                    side = 0 if i == 0 else 1
                    tile = edge_value(2, side, j, face(s), *far_pair)
                else:
                    tile = conv[2, i, j, face(s)] * fluid
                packs = pack_entry(packs, tile, i * order + j, s)
        send2_z[s] = packs
    each(pick(round2, 2), "start")

    def whole_x(c):
        each(pick(round1x, c), "arrive")
        far = split_x(strip_x.at[c], range(order))
        for j, k in far:
            far_x[c, j, k] = far[j, k]

    whole_x(0)
    face_terms(0, 0, ends)
    advance(0, ends)
    for j in range(order):
        for k in range(order):
            top2_x[j, k] = roll(conv[0, order - 1, j, k], ey - rows, 0)
    each(pick(round2, 0), "start")

    face_terms(2, 1, ends)
    far_e = [split_x(strip_e.at[c], ends) for c in range(2)]
    for s in range(2):
        for k in range(order):
            far_pair = far_e[0][face(s), k], far_e[1][face(s), k]
            for i in range(order):
                if i in ends:
                    side = 0 if i == 0 else 1
                    send2_y[s, i, k] = edge_value(1, side, face(s), k, *far_pair)
                else:
                    send2_y[s, i, k] = conv[1, i, face(s), k] * fluid
    each(pick(round2, 1), "start")

    merge_y(0, middle)
    turn_y(0, middle, whole)
    turn_y(2, whole, middle)
    for c in range(3):
        inner(c, middle)
        for a in (1, 2):
            if a != c:
                face_terms(a, c, middle)
    advance(0, middle)
    for c in x_order[1:]:
        whole_x(c)
        face_terms(0, c, range(order))
        advance(c, range(order))

    hats = hat_weight_table()
    slopes = lobatto_weights() / 2

    def hat_pair(lines):
        e1, e2 = lines[0] + lines[4], lines[1] + lines[3]
        whole_sum = mix(
            (hats[0, 0] + hats[0, 4], hats[0, 1] + hats[0, 3], hats[0, 2] * 2), (e1, e2, lines[2])
        )
        d1, d2 = lines[4] - lines[0], lines[3] - lines[1]
        gap = mix((hats[0, 0] - hats[0, 4], hats[0, 1] - hats[0, 3]), (d1, d2))
        return (0.5 * (whole_sum - gap), 0.5 * (whole_sum + gap))

    def plane(get):
        along = [hat_pair([get(p, q) for q in range(order)]) for p in range(order)]
        return [
            list(pair)
            for pair in zip(*[hat_pair([along[p][b] for p in range(order)]) for b in range(2)])
        ]

    parts = {}
    for a in range(3):

        def slope(p, q):
            f = [conv[(a,) + node(a, l, p, q)] for l in range(order)]
            return mix(slopes[:3], (f[0] + f[4], f[1] + f[3], f[2]))

        inside = plane(slope)
        bottom = plane(lambda p, q: conv[(a,) + node(a, 0, p, q)])
        open_end = jnp.where(jnp.logical_and(edges[a][0], me[a] == 0), 0.5, 0.0)
        for p in range(2):
            for q in range(2):
                for b in range(2):
                    key = node(a, b, p, q)
                    piece = inside[p][q] if b == 1 else open_end * bottom[p][q] - inside[p][q]
                    parts[key] = parts[key] + piece if key in parts else piece
    for a in (2, 1, 0):
        edge = edges[a][0]
        merged = {}
        for key in parts:
            if key[a] == 1:
                continue
            upper = key[:a] + (1,) + key[a + 1 :]
            moved = brick.move(parts[upper], a, True)
            if a == 1:
                moved = jnp.where(edge, roll(parts[upper], 1 - ey, 0), moved)
            merged[key] = parts[key] + jnp.where(edge, 0.0, moved)
            merged[upper] = jnp.where(edge, moved, 0.0)
        parts = merged
    for n, shift in enumerate(corners):
        send3[n] = parts[shift]
    each(round3, "start")
    each(round1x, "finish")
    each(round1e, "finish")
    each(round1, "finish")

    for a in range(3):
        for p in range(order):
            for q in range(order):
                out = lifted_derivative(
                    [conv[(a,) + node(a, l, p, q)] for l in range(order)], -1.0
                )
                for l in range(order):
                    where = node(a, l, p, q)
                    pres[where] = out[l] if a == 0 else pres[where] + out[l]

    eigen = eigen_value_table()
    slot_of = {}
    for key in itertools.combinations_with_replacement(range(order), 3):
        slot_of[key] = len(slot_of)
        size = float(np.prod([norm_squares[k] for k in key]))
        inverse[slot_of[key]] = 1.0 / (scale * float(sum(eigen[k] for k in key) / size) + 1.0 / size)

    def far_faces(a):
        each(pick(round2, a), "arrive")
        for s in range(2):
            own = order - 1 - face(s)
            for p in range(order):
                for q in range(order):
                    if a == 0:
                        far = far2_x[s, p, q]
                        far = far if s == 0 else roll(far, rows - ey, 0)
                    elif a == 1:
                        far = far2_y[s, p, q]
                    else:
                        far = unpack_entry(far2_z[s], p * order + q, s)
                    inside = brick.move(conv[(a,) + node(a, face(s), p, q)], a, s == 0)
                    side = half_lift * jnp.where(edges[a][s], far, inside)
                    where = node(a, own, p, q)
                    pres[where] = pres[where] + side if s == 0 else pres[where] - side

    span = range(order)

    def layer_modes(i):
        grid = [to_modes([pres[i, j, k] for k in span]) for j in span]
        cols = [to_modes([grid[j][k] for j in span]) for k in span]
        for j in span:
            for k in span:
                pres[i, j, k] = cols[k][j]

    far_faces(2)
    far_faces(1)
    for i in middle:
        layer_modes(i)
    far_faces(0)
    for i in ends:
        layer_modes(i)
    for j in span:
        for k in span:
            modes = to_modes([pres[i, j, k] for i in span])
            modes = [modes[i] * inverse[slot_of[tuple(sorted((i, j, k)))]] for i in span]
            out = from_modes(modes)
            for i in span:
                pres[i, j, k] = out[i]

    def turned(batch):
        for i in batch:
            for j in span:
                out = from_modes([pres[i, j, k] for k in span])
                for k in span:
                    pres[i, j, k] = out[k]
        for k in span:
            index = ((lane + (ez - k)) * spread) % ez
            for i in batch:
                for j in span:
                    pres[i, j, k] = permute(pres[i, j, k], index)

    def written(batch):
        for i in batch:
            for j in span:
                mixed = [None] * order
                for k in span:
                    mixed[(turn * k) % order] = pres[i, j, k]
                natural = barrel(mixed, -1)
                for t in span:
                    pres[i, j, t] = natural[t]
            for t in span:
                out = from_modes([pres[i, j, t] for j in span])
                for j in span:
                    for x in range(ex):
                        out_ref[i, t, pl.ds(x * pitch + j, ey, stride=order), :] = out[j][
                            x * ey : (x + 1) * ey
                        ]

    batches = ((0, 1), (2, 3), (4,))
    turned(batches[0])
    for n in range(1, len(batches)):
        turned(batches[n])
        written(batches[n - 1])
    written(batches[-1])

    each(round2, "finish")
    each(round3, "arrive")
    total = parts[(0, 0, 0)]
    for n in range(len(corners)):
        total = total + recv3[n]
    for x in range(ex):
        coarse_ref[x] = total[x * ey : (x + 1) * ey]
    each(round3, "finish")


def deliver(brick, packed_ref, part_ref, smooth_ref, coarse_ref, sems):
    ez, ny, pitch = brick.ez, brick.ny, brick.pitch
    copies = [pltpu.make_async_copy(part_ref, coarse_ref, sems.at[0])]
    for x in range(brick.ex):
        for t in range(order):
            copies.append(
                pltpu.make_async_copy(
                    packed_ref.at[:, t, x * pitch : x * pitch + ny],
                    smooth_ref.at[x * order : (x + 1) * order, :, t * ez : (t + 1) * ez],
                    sems.at[len(copies)],
                )
            )
    for copy in copies:
        copy.start()
    for copy in copies:
        copy.wait()


def shards(counts, velocity, mask, scale):
    ex, ey, ez = mask.shape
    brick = Brick(ex, ey, ez)
    tile = (brick.rows, ez)
    f32 = jnp.float32
    whole = pl.BlockSpec(memory_space=pltpu.VMEM)
    remote = pl.BlockSpec(memory_space=pltpu.HBM)
    sems = pltpu.SemaphoreType.DMA
    lines = (order, order)
    strips = (order, order, ex * brick.pitch, ez)
    triples = len(list(itertools.combinations_with_replacement(range(order), 3)))
    pairs = [(2,), (2,)]
    for n in (2, 2, 6, 2, 2, 2, 2, 2, len(corners)):
        pairs += [(n,), (n,)]

    def vmem(*shape):
        return pltpu.VMEM(shape, f32)

    packed, part = pl.pallas_call(
        functools.partial(body, brick, counts),
        out_shape=(
            jax.ShapeDtypeStruct(strips, f32),
            jax.ShapeDtypeStruct(mask.shape, f32),
        ),
        in_specs=[remote] * 3,
        out_specs=(whole, whole),
        scratch_shapes=[
            vmem(3, *strips),
            pltpu.VMEM(mask.shape, jnp.int32),
            vmem(*scale.shape),
            vmem(3, order, *lines, *tile),
            vmem(3, order, *lines, *tile),
            vmem(3, *strips[1:]),
            vmem(2, *strips[1:]),
            vmem(2, 2, *tile),
            vmem(2, *lines, *tile),
            vmem(3, *lines, *tile),
            vmem(3, *lines, *tile),
            vmem(3, *lines, *tile),
            vmem(2, *tile),
            vmem(2, *tile),
            vmem(2, 3, *lines, *tile),
            vmem(3, 2, 2, *lines, *tile),
            vmem(order, *lines, *tile),
            vmem(triples, *tile),
            vmem(*lines, *tile),
            vmem(2, *lines, *tile),
            vmem(2, *lines, *tile),
            vmem(2, *tile),
            vmem(2, *tile),
            vmem(len(corners), *tile),
            vmem(len(corners), *tile),
        ]
        + [sems(shape) for shape in pairs],
        compiler_params=pltpu.CompilerParams(
            collective_id=0, has_side_effects=True, vmem_limit_bytes=32 << 20
        ),
    )(*[pltpu.with_memory_space_constraint(z, pltpu.HBM) for z in (velocity, mask, scale)])
    return pl.pallas_call(
        functools.partial(deliver, brick),
        out_shape=(
            jax.ShapeDtypeStruct(velocity.shape[1:], f32),
            jax.ShapeDtypeStruct(mask.shape, f32),
        ),
        in_specs=[whole] * 2,
        out_specs=(remote, remote),
        scratch_shapes=[sems((1 + ex * order,))],
        compiler_params=pltpu.CompilerParams(vmem_limit_bytes=16 << 20),
    )(packed, part)


def solution(mesh):
    counts = tuple(mesh.shape[name] for name in names)
    return jax.shard_map(
        functools.partial(shards, counts),
        mesh=mesh,
        in_specs=(P(None, "gx", "gy", "gz"), P("gx", "gy", "gz"), P("gx", "gy", "gz")),
        out_specs=(P("gx", "gy", "gz"), P("gx", "gy", "gz")),
        check_vma=False,
    )
```

```python
import functools
import itertools
import math

import jax
import jax.numpy as jnp
import numpy as np
from jax import lax
from jax.experimental import pallas as pl
from jax.experimental.pallas import tpu as pltpu
from jax.sharding import PartitionSpec as P

lift_factor = 10.0
time_step = 0.05
penalty = 4.0
half_lift = lift_factor * 0.5
order = 5
names = ("gx", "gy", "gz")
corners = [s for s in itertools.product((0, 1), repeat=3) if any(s)]
x_order = (0, 2, 1)


def lobatto_points():
    return np.array([-1.0, -math.sqrt(3.0 / 7.0), 0.0, math.sqrt(3.0 / 7.0), 1.0])


def lobatto_weights():
    return np.array([0.1, 49.0 / 90.0, 32.0 / 45.0, 49.0 / 90.0, 0.1])


def derivative_matrix():
    points = lobatto_points()
    scales = np.array(
        [np.prod([points[i] - points[k] for k in range(5) if k != i]) for i in range(5)]
    )
    result = np.zeros((5, 5))
    for i in range(5):
        for j in range(5):
            if i != j:
                result[i, j] = scales[i] / (scales[j] * (points[i] - points[j]))
        result[i, i] = -np.sum(result[i])
    return result


def eigen_value_table():
    return np.array([4.0 * math.sin(math.pi * k / 10.0) ** 2 for k in range(5)])


def hat_weight_table():
    points = lobatto_points()
    weights = lobatto_weights()
    return np.array([weights * (1.0 - points) / 2.0, weights * (1.0 + points) / 2.0])


def mix(coefs, terms):
    total = None
    for coef, term in zip(coefs, terms):
        if abs(coef) < 1e-12:
            continue
        piece = float(coef) * term
        total = piece if total is None else total + piece
    return total


def lifted_derivative(f, factor):
    d = derivative_matrix()
    d[0, 0] += half_lift
    d[4, 4] -= half_lift
    d = d * factor
    e1, e2 = f[0] + f[4], f[1] + f[3]
    o1, o2 = f[0] - f[4], f[1] - f[3]
    out = [None] * 5
    for i in range(2):
        even = mix(((d[i, 0] + d[i, 4]) / 2, (d[i, 1] + d[i, 3]) / 2, d[i, 2]), (e1, e2, f[2]))
        odd = mix(((d[i, 0] - d[i, 4]) / 2, (d[i, 1] - d[i, 3]) / 2), (o1, o2))
        out[i] = odd + even
        out[4 - i] = odd - even
    out[2] = mix((d[2, 0], d[2, 1]), (o1, o2))
    return out


cos18, cos54 = math.cos(math.pi * 0.1), math.cos(math.pi * 0.3)
cos36, cos72 = math.cos(math.pi * 0.2), math.cos(math.pi * 0.4)
even_gain = (cos36 + cos72) / 2
odd_ratio = cos54 / cos18
norm_squares = [0.2, 0.4 * cos18**2, 0.4, 0.4 * cos18**2, 0.4]


def to_modes(f):
    e1, e2 = f[0] + f[4], f[1] + f[3]
    o1, o2 = f[0] - f[4], f[1] - f[3]
    s = e1 + e2
    p = even_gain * (e1 - e2)
    q = 0.25 * s - f[2]
    return [s + f[2], o1 + odd_ratio * o2, p + q, odd_ratio * o1 - o2, p - q]


def from_modes(c):
    s, d = c[2] + c[4], c[2] - c[4]
    p = even_gain * s
    base = c[0] + 0.25 * d
    even = (base + p, base - p)
    odd = (c[1] + odd_ratio * c[3], odd_ratio * c[1] - c[3])
    return [even[0] + odd[0], even[1] + odd[1], c[0] - d, even[1] - odd[1], even[0] - odd[0]]


def roll(x, shift, axis):
    size = x.shape[axis]
    shift = shift % size
    return x if shift == 0 else pltpu.roll(x, shift, axis)


class Brick:
    def __init__(self, ex, ey, ez):
        self.ex, self.ey, self.ez = ex, ey, ez
        self.rows = ex * ey
        self.ny = ey * order
        self.pitch = -(-self.ny // 8) * 8

    def iotas(self):
        row = lax.broadcasted_iota(jnp.int32, (self.rows, self.ez), 0)
        lane = lax.broadcasted_iota(jnp.int32, (self.rows, self.ez), 1)
        return row, lane

    def slots(self, a):
        return (self.ex, self.ey, self.ez)[a]

    def place(self, a):
        row, lane = self.iotas()
        return (row // self.ey, row % self.ey, lane)[a]

    def move(self, x, a, up):
        step = (self.ey, 1, 1)[a]
        return roll(x, step if up else -step, x.ndim - (1 if a == 2 else 2))

    def edge(self, a, up):
        return self.place(a) == (0 if up else self.slots(a) - 1)


def body(
    brick,
    counts,
    v_ref,
    mask_ref,
    scale_ref,
    out_ref,
    coarse_ref,
    raw,
    mask_buf,
    scale_buf,
    vel,
    conv,
    strip_x,
    strip_e,
    far_zx,
    send2_y,
    raw_y,
    far_x,
    far_y,
    send_z,
    far_z,
    shifted,
    gain,
    pres,
    inverse,
    top2_x,
    far2_x,
    far2_y,
    send2_z,
    far2_z,
    send3,
    recv3,
    *sems,
):
    (load_sem, small_sem, se, re, szx, rzx, sx, rx, sy, ry, sz, rz, s2x, r2x, s2y, r2y, s2z, r2z, s3, r3) = sems
    ex, ey, ez, rows, ny, pitch = brick.ex, brick.ey, brick.ez, brick.rows, brick.ny, brick.pitch
    me = [lax.axis_index(name) for name in names]
    ends, middle = (0, order - 1), tuple(range(1, order - 1))

    def exists(shift):
        ok = None
        for a in range(3):
            if shift[a] > 0:
                one = me[a] < counts[a] - 1
            elif shift[a] < 0:
                one = me[a] > 0
            else:
                continue
            ok = one if ok is None else jnp.logical_and(ok, one)
        return ok

    def device(shift):
        return tuple(me[a] + shift[a] for a in range(3))

    unit = [tuple(int(a == b) for b in range(3)) for a in range(3)]

    def toward(a, s):
        return tuple((1 - 2 * s) * u for u in unit[a])

    partners = [toward(a, s) for a in range(3) for s in range(2)]
    greeted = partners + [(-1, -1, -1)]
    awaited = partners + [(1, 1, 1)]
    barrier = pltpu.get_barrier_semaphore()
    for shift in greeted:

        @pl.when(exists(shift))
        def _():
            pl.semaphore_signal(
                barrier, inc=1, device_id=device(shift), device_id_type=pl.DeviceIdType.MESH
            )

    for t in ends + middle:
        for x in range(ex):
            pltpu.make_async_copy(
                v_ref.at[:, x * order : (x + 1) * order, :, t * ez : (t + 1) * ez],
                raw.at[:, :, t, x * pitch : x * pitch + ny],
                load_sem.at[0 if t in ends else 1],
            ).start()
    small = [
        pltpu.make_async_copy(mask_ref, mask_buf, small_sem.at[0]),
        pltpu.make_async_copy(scale_ref, scale_buf, small_sem.at[1]),
    ]
    for copy in small:
        copy.start()

    def loaded(group):
        landed = raw.at[:, :, 0 : (2, order - 2)[group], 0 : ex * ny]
        pltpu.make_async_copy(landed, landed, load_sem.at[group]).wait()

    class Group:
        def __init__(self, shift, pairs, ssem, rsem, dst, whole=None):
            self.to, self.source = exists(shift), exists(tuple(-x for x in shift))
            self.dst = dst
            self.copies = [self.copy(src, to, ssem, rsem, shift) for src, to in pairs]
            self.all = self.copies[0] if whole is None else self.copy(whole, whole, ssem, rsem, shift)

        def copy(self, src, dst, ssem, rsem, shift):
            return pltpu.make_async_remote_copy(
                src_ref=src,
                dst_ref=dst,
                send_sem=ssem,
                recv_sem=rsem,
                device_id=device(shift),
                device_id_type=pl.DeviceIdType.MESH,
            )

        def start(self):
            @pl.when(self.to)
            def _():
                for copy in self.copies:
                    copy.start()

        def clear(self):
            @pl.when(jnp.logical_not(self.source))
            def _():
                self.dst[...] = jnp.zeros_like(self.dst)

        def arrive(self):
            @pl.when(self.source)
            def _():
                self.all.wait_recv()

        def finish(self):
            @pl.when(self.to)
            def _():
                self.all.wait_send()

    def y_rows(s):
        return [
            (x * ey + ey - 1, x * ey) if s == 0 else (x * ey, x * ey + ey - 1) for x in range(ex)
        ]

    def face(s):
        return order - 1 if s == 0 else 0

    round1x, round1e, round1, round2, round3 = {}, {}, {}, {}, {}
    for s in range(2):
        for c in range(3):
            n = c * 2 + s
            x, to = (ex - 1, 0) if s == 0 else (0, ex - 1)
            round1x[c, s] = Group(
                toward(0, s),
                [
                    (
                        raw.at[c, face(s), :, x * pitch : x * pitch + ny],
                        strip_x.at[c, :, to * pitch : to * pitch + ny],
                    )
                ],
                sx.at[n],
                rx.at[n],
                None,
            )
        round1e[0, s] = Group(
            toward(0, s),
            [
                (raw.at[0:2, face(s), :, x * pitch + r], strip_e.at[:, :, to * pitch + r])
                for r in (0, ny - 1)
            ],
            se.at[s],
            re.at[s],
            None,
            strip_e.at[:, :, 0:2],
        )
        round1e[1, s] = Group(
            toward(0, s), [(send_z, far_zx.at[s])], szx.at[s], rzx.at[s], None
        )
        line = ny - 1 if s == 0 else 0
        round1[1, s] = Group(
            toward(1, s),
            [
                (raw.at[:, :, :, x * pitch + line], raw_y.at[:, :, :, dst])
                for x, (_, dst) in enumerate(y_rows(s))
            ],
            sy.at[s],
            ry.at[s],
            None,
            raw_y.at[:, :, :, 0:ex],
        )
        round1[2, s] = Group(
            toward(2, s), [(send_z.at[s], far_z.at[s])], sz.at[s], rz.at[s], None
        )
        src = top2_x if s == 0 else conv.at[0, 0]
        round2[0, s] = Group(
            toward(0, s),
            [(src.at[:, :, 0:ey], far2_x.at[s, :, :, 0:ey])],
            s2x.at[s],
            r2x.at[s],
            far2_x.at[s],
        )
        round2[1, s] = Group(
            toward(1, s),
            [
                (send2_y.at[s, :, :, src], far2_y.at[s, :, :, dst])
                for src, dst in y_rows(s)
            ],
            s2y.at[s],
            r2y.at[s],
            far2_y.at[s],
            far2_y.at[s, :, :, 0:ex],
        )
        round2[2, s] = Group(
            toward(2, s), [(send2_z.at[s], far2_z.at[s])], s2z.at[s], r2z.at[s], far2_z.at[s]
        )
    for n, shift in enumerate(corners):
        round3[n] = Group(shift, [(send3.at[n], recv3.at[n])], s3.at[n], r3.at[n], recv3.at[n])

    def each(groups, act):
        for key in groups:
            getattr(groups[key], act)()

    def pick(groups, a):
        return {key: groups[key] for key in groups if key[0] == a}

    row, lane = brick.iotas()
    spread = pow(order, -1, ez)
    turn = pow(ez, -1, order)
    phase = (turn * lane) % order
    bits = [(phase & bit) != 0 for bit in (1, 2, 4)]
    place_x = brick.place(0)
    edges = [[brick.edge(a, s == 0) for s in range(2)] for a in range(3)]
    zero = jnp.zeros((rows, ez), jnp.float32)

    def known(a):
        here = [jnp.logical_and(edges[a][s], exists(toward(a, 1 - s))) for s in range(2)]
        return jnp.logical_or(*here)

    def permute(x, index):
        return jnp.take_along_axis(x, index, axis=1, mode="promise_in_bounds")

    def barrel(tiles, sign):
        for bit, on in zip((1, 2, 4), bits):
            tiles = [jnp.where(on, tiles[(m - sign * bit) % order], tiles[m]) for m in range(order)]
        return tiles

    def split_index(k):
        return (lane * order + k) % ez

    def pack_entry(total, tile, n, s):
        start = ez - 1 if s == 0 else 0
        return jnp.where(lane == n, roll(tile, n - start, 1), total)

    def unpack_entry(packed, n, s):
        return roll(packed, (0 if s == 0 else ez - 1) - n, 1)

    def fetch(strip, j):
        tile = None
        for x in range(ex):
            part = strip[pl.ds(j + x * (pitch - ny), rows, stride=order), :]
            tile = part if x == 0 else jnp.where(place_x == x, part, tile)
        return tile

    loaded(0)
    for s in range(2):
        packs = zero
        for n in range(3 * order * order):
            c, i, j = n // order**2, n // order % order, n % order
            packs = pack_entry(packs, fetch(raw.at[c, i, face(s)], j), n, s)
        send_z[s] = packs

    loaded(1)
    pl.semaphore_wait(barrier, sum(exists(shift).astype(jnp.int32) for shift in awaited))
    each(round1e, "start")
    each(pick(round1, 2), "start")
    each(pick(round1x, 0), "start")
    each(pick(round1, 1), "start")
    for c in x_order[1:]:
        each(pick(round1x, c), "start")

    def gather(c, i):
        for j in range(order):
            merged = barrel([fetch(raw.at[c, i, t], j) for t in range(order)], 1)
            for k in range(order):
                vel[c, i, j, k] = merged[(turn * k) % order]

    def scatter(c, k):
        for i in range(order):
            for j in range(order):
                vel[c, i, j, k] = permute(vel[c, i, j, k], split_index(k))

    for i in range(order):
        gather(x_order[0], i)
    for n, c in enumerate(x_order):
        for k in range(order):
            scatter(c, k)
            if n < 2:
                gather(x_order[n + 1], k)

    each(round2, "clear")
    each(round3, "clear")

    def node(a, l, p, q):
        return ((l, p, q), (p, l, q), (p, q, l))[a]

    def lines(a, c, wanted):
        pairs = itertools.product(range(order), repeat=2)
        return [pq for pq in pairs if a == c or node(a, 0, *pq)[c] in wanted]

    def inner(c, wanted):
        for a in (c,) + tuple(b for b in range(3) if b != c):
            for p, q in lines(a, c, wanted):
                normal = [vel[(a,) + node(a, l, p, q)] for l in range(order)]
                moved = normal
                if a != c:
                    moved = [vel[(c,) + node(a, l, p, q)] for l in range(order)]
                out = lifted_derivative([n * w for n, w in zip(normal, moved)], -time_step)
                for l in wanted if a == c else range(order):
                    where = (c,) + node(a, l, p, q)
                    conv[where] = (moved[l] if a == c else conv[where]) + out[l]

    for c in x_order:
        inner(c, ends)
    for s in range(2):
        for c in range(3):
            for p in range(order):
                for q in range(order):
                    shifted[s, c, p, q] = brick.move(vel[c, p, q, face(s)], 2, s == 0)

    for copy in small:
        copy.wait()
    solid = jnp.concatenate([mask_buf[x] for x in range(ex)], axis=0).astype(jnp.float32)
    scale = jnp.concatenate([scale_buf[x] for x in range(ex)], axis=0)
    fluid = 1.0 / (1.0 + penalty * solid)

    def near(a, s, c, p, q):
        if a == 2:
            far = unpack_entry(far_z[s], (c * order + p) * order + q, s)
            far = jnp.where(exists(toward(2, 1 - s)), far, zero)
            return jnp.where(edges[2][s], far, shifted[s, c, p, q])
        far = far_x[c, p, q] if a == 0 else far_y[c, p, q]
        inside = brick.move(vel[(c,) + node(a, face(s), p, q)], a, s == 0)
        return jnp.where(edges[a][s], far, inside)

    step_lift = time_step * half_lift

    def face_terms(a, c, wanted):
        for s in range(2):
            own = order - 1 - face(s)
            for p, q in lines(a, c, wanted):
                where = (c,) + node(a, own, p, q)
                moved, moved_out = vel[where], near(a, s, c, p, q)
                if a == c:
                    down = step_lift * jnp.maximum(jnp.abs(moved), jnp.abs(moved_out))
                    flow = step_lift * moved_out
                    across = down + flow if s == 0 else down - flow
                    gain[a, s, 0, p, q] = across
                    gain[a, s, 1, p, q] = down
                else:
                    across, down = gain[a, s, 0, p, q], gain[a, s, 1, p, q]
                conv[where] = conv[where] + (across * moved_out - down * moved)

    def advance(c, wanted):
        for l in wanted:
            for p in range(order):
                for q in range(order):
                    where = (c,) + node(c, l, p, q)
                    conv[where] = conv[where] * fluid

    each(round1, "arrive")
    each(round1e, "arrive")
    valid = known(1)

    def merge_y(c, todo):
        for i in todo:
            mixed = barrel([jnp.where(valid, raw_y[c, i, t], zero) for t in range(order)], 1)
            for k in range(order):
                far_y[c, i, k] = mixed[(turn * k) % order]

    def turn_y(c, todo, planes):
        for k in planes:
            for i in todo:
                far_y[c, i, k] = permute(far_y[c, i, k], split_index(k))

    whole = range(order)
    merge_y(1, whole)
    merge_y(0, ends)
    merge_y(2, whole)
    for k in whole:
        turn_y(1, whole, (k,))
        turn_y(0, ends, (k,))
        if k in ends:
            turn_y(2, whole, (k,))
    face_terms(2, 2, ends)
    face_terms(2, 0, ends)
    face_terms(1, 1, ends)
    face_terms(1, 2, ends)
    face_terms(1, 0, ends)

    valid_x = known(0)

    def split_x(strip, todo):
        mixed = {}
        for j in todo:
            natural = [jnp.where(valid_x, fetch(strip.at[t], j), zero) for t in range(order)]
            mixed[j] = barrel(natural, 1)
        return {
            (j, k): permute(mixed[j][(turn * k) % order], split_index(k))
            for k in range(order)
            for j in todo
        }

    def edge_value(c, s, j, k, far_normal, far_moved):
        own = order - 1 - face(s)

        def outside(b, far):
            return jnp.where(edges[0][s], far, brick.move(vel[b, face(s), j, k], 0, s == 0))

        normal, normal_out = vel[0, own, j, k], outside(0, far_normal)
        down = step_lift * jnp.maximum(jnp.abs(normal), jnp.abs(normal_out))
        flow = step_lift * normal_out
        across = down + flow if s == 0 else down - flow
        term = across * outside(c, far_moved) - down * vel[c, own, j, k]
        return (conv[c, own, j, k] + term) * fluid

    packed_ends = []
    for s in range(2):
        low = roll(far_zx[0, s], -(ex - 1) * ey, 0)
        high = roll(roll(far_zx[1, s], (ex - 1) * ey, 0), (order - 1) * order, 1)
        packed_ends.append(jnp.where(valid_x, jnp.where(place_x == 0, low, high), zero))

    def far_end(c, j, s):
        n = (c * order + order - 1) * order + j
        return roll(packed_ends[s], (ez - 1 if s == 0 else 0) - n, 1)

    for s in range(2):
        packs = zero
        for j in range(order):
            far_pair = far_end(0, j, s), far_end(2, j, s)
            for i in range(order):
                if i in ends:
                    side = 0 if i == 0 else 1
                    tile = edge_value(2, side, j, face(s), *far_pair)
                else:
                    tile = conv[2, i, j, face(s)] * fluid
                packs = pack_entry(packs, tile, i * order + j, s)
        send2_z[s] = packs
    each(pick(round2, 2), "start")

    def whole_x(c):
        each(pick(round1x, c), "arrive")
        far = split_x(strip_x.at[c], range(order))
        for j, k in far:
            far_x[c, j, k] = far[j, k]

    whole_x(0)
    face_terms(0, 0, ends)
    advance(0, ends)
    for j in range(order):
        for k in range(order):
            top2_x[j, k] = roll(conv[0, order - 1, j, k], ey - rows, 0)
    each(pick(round2, 0), "start")

    face_terms(2, 1, ends)
    far_e = [split_x(strip_e.at[c], ends) for c in range(2)]
    for s in range(2):
        for k in range(order):
            far_pair = far_e[0][face(s), k], far_e[1][face(s), k]
            for i in range(order):
                if i in ends:
                    side = 0 if i == 0 else 1
                    send2_y[s, i, k] = edge_value(1, side, face(s), k, *far_pair)
                else:
                    send2_y[s, i, k] = conv[1, i, face(s), k] * fluid
    each(pick(round2, 1), "start")

    merge_y(0, middle)
    turn_y(0, middle, whole)
    turn_y(2, whole, middle)
    for c in range(3):
        inner(c, middle)
        for a in (1, 2):
            if a != c:
                face_terms(a, c, middle)
    advance(0, middle)
    for c in x_order[1:]:
        whole_x(c)
        face_terms(0, c, range(order))
        advance(c, range(order))

    hats = hat_weight_table()
    slopes = lobatto_weights() / 2

    def hat_pair(lines):
        e1, e2 = lines[0] + lines[4], lines[1] + lines[3]
        whole_sum = mix(
            (hats[0, 0] + hats[0, 4], hats[0, 1] + hats[0, 3], hats[0, 2] * 2), (e1, e2, lines[2])
        )
        d1, d2 = lines[4] - lines[0], lines[3] - lines[1]
        gap = mix((hats[0, 0] - hats[0, 4], hats[0, 1] - hats[0, 3]), (d1, d2))
        return (0.5 * (whole_sum - gap), 0.5 * (whole_sum + gap))

    def plane(get):
        along = [hat_pair([get(p, q) for q in range(order)]) for p in range(order)]
        return [
            list(pair)
            for pair in zip(*[hat_pair([along[p][b] for p in range(order)]) for b in range(2)])
        ]

    parts = {}
    for a in range(3):

        def slope(p, q):
            f = [conv[(a,) + node(a, l, p, q)] for l in range(order)]
            return mix(slopes[:3], (f[0] + f[4], f[1] + f[3], f[2]))

        inside = plane(slope)
        bottom = plane(lambda p, q: conv[(a,) + node(a, 0, p, q)])
        open_end = jnp.where(jnp.logical_and(edges[a][0], me[a] == 0), 0.5, 0.0)
        for p in range(2):
            for q in range(2):
                for b in range(2):
                    key = node(a, b, p, q)
                    piece = inside[p][q] if b == 1 else open_end * bottom[p][q] - inside[p][q]
                    parts[key] = parts[key] + piece if key in parts else piece
    for a in (2, 1, 0):
        edge = edges[a][0]
        merged = {}
        for key in parts:
            if key[a] == 1:
                continue
            upper = key[:a] + (1,) + key[a + 1 :]
            moved = brick.move(parts[upper], a, True)
            if a == 1:
                moved = jnp.where(edge, roll(parts[upper], 1 - ey, 0), moved)
            merged[key] = parts[key] + jnp.where(edge, 0.0, moved)
            merged[upper] = jnp.where(edge, moved, 0.0)
        parts = merged
    for n, shift in enumerate(corners):
        send3[n] = parts[shift]
    each(round3, "start")
    each(round1x, "finish")
    each(round1e, "finish")
    each(round1, "finish")

    for a in range(3):
        for p in range(order):
            for q in range(order):
                out = lifted_derivative(
                    [conv[(a,) + node(a, l, p, q)] for l in range(order)], -1.0
                )
                for l in range(order):
                    where = node(a, l, p, q)
                    pres[where] = out[l] if a == 0 else pres[where] + out[l]

    eigen = eigen_value_table()
    slot_of = {}
    for key in itertools.combinations_with_replacement(range(order), 3):
        slot_of[key] = len(slot_of)
        size = float(np.prod([norm_squares[k] for k in key]))
        inverse[slot_of[key]] = 1.0 / (scale * float(sum(eigen[k] for k in key) / size) + 1.0 / size)

    def far_faces(a):
        each(pick(round2, a), "arrive")
        for s in range(2):
            own = order - 1 - face(s)
            for p in range(order):
                for q in range(order):
                    if a == 0:
                        far = far2_x[s, p, q]
                        far = far if s == 0 else roll(far, rows - ey, 0)
                    elif a == 1:
                        far = far2_y[s, p, q]
                    else:
                        far = unpack_entry(far2_z[s], p * order + q, s)
                    inside = brick.move(conv[(a,) + node(a, face(s), p, q)], a, s == 0)
                    side = half_lift * jnp.where(edges[a][s], far, inside)
                    where = node(a, own, p, q)
                    pres[where] = pres[where] + side if s == 0 else pres[where] - side

    span = range(order)

    def layer_modes(i):
        grid = [to_modes([pres[i, j, k] for k in span]) for j in span]
        cols = [to_modes([grid[j][k] for j in span]) for k in span]
        for j in span:
            for k in span:
                pres[i, j, k] = cols[k][j]

    far_faces(2)
    far_faces(1)
    for i in middle:
        layer_modes(i)
    far_faces(0)
    for i in ends:
        layer_modes(i)
    for j in span:
        for k in span:
            modes = to_modes([pres[i, j, k] for i in span])
            modes = [modes[i] * inverse[slot_of[tuple(sorted((i, j, k)))]] for i in span]
            out = from_modes(modes)
            for i in span:
                pres[i, j, k] = out[i]

    def turned(batch):
        for i in batch:
            for j in span:
                out = from_modes([pres[i, j, k] for k in span])
                for k in span:
                    pres[i, j, k] = out[k]
        for k in span:
            index = ((lane + (ez - k)) * spread) % ez
            for i in batch:
                for j in span:
                    pres[i, j, k] = permute(pres[i, j, k], index)

    def written(batch):
        for i in batch:
            for j in span:
                mixed = [None] * order
                for k in span:
                    mixed[(turn * k) % order] = pres[i, j, k]
                natural = barrel(mixed, -1)
                for t in span:
                    pres[i, j, t] = natural[t]
            for t in span:
                out = from_modes([pres[i, j, t] for j in span])
                for j in span:
                    for x in range(ex):
                        out_ref[i, t, pl.ds(x * pitch + j, ey, stride=order), :] = out[j][
                            x * ey : (x + 1) * ey
                        ]

    batches = ((0, 1), (2, 3), (4,))
    turned(batches[0])
    for n in range(1, len(batches)):
        turned(batches[n])
        written(batches[n - 1])
    written(batches[-1])

    each(round2, "finish")
    each(round3, "arrive")
    total = parts[(0, 0, 0)]
    for n in range(len(corners)):
        total = total + recv3[n]
    for x in range(ex):
        coarse_ref[x] = total[x * ey : (x + 1) * ey]
    each(round3, "finish")


def deliver(brick, packed_ref, part_ref, smooth_ref, coarse_ref, sems):
    ez, ny, pitch = brick.ez, brick.ny, brick.pitch
    copies = [pltpu.make_async_copy(part_ref, coarse_ref, sems.at[0])]
    for x in range(brick.ex):
        for t in range(order):
            copies.append(
                pltpu.make_async_copy(
                    packed_ref.at[:, t, x * pitch : x * pitch + ny],
                    smooth_ref.at[x * order : (x + 1) * order, :, t * ez : (t + 1) * ez],
                    sems.at[len(copies)],
                )
            )
    for copy in copies:
        copy.start()
    for copy in copies:
        copy.wait()


def shards(counts, velocity, mask, scale):
    ex, ey, ez = mask.shape
    brick = Brick(ex, ey, ez)
    tile = (brick.rows, ez)
    f32 = jnp.float32
    whole = pl.BlockSpec(memory_space=pltpu.VMEM)
    remote = pl.BlockSpec(memory_space=pltpu.HBM)
    sems = pltpu.SemaphoreType.DMA
    lines = (order, order)
    strips = (order, order, ex * brick.pitch, ez)
    triples = len(list(itertools.combinations_with_replacement(range(order), 3)))
    pairs = [(2,), (2,)]
    for n in (2, 2, 6, 2, 2, 2, 2, 2, len(corners)):
        pairs += [(n,), (n,)]

    def vmem(*shape):
        return pltpu.VMEM(shape, f32)

    packed, part = pl.pallas_call(
        functools.partial(body, brick, counts),
        out_shape=(
            jax.ShapeDtypeStruct(strips, f32),
            jax.ShapeDtypeStruct(mask.shape, f32),
        ),
        in_specs=[remote] * 3,
        out_specs=(whole, whole),
        scratch_shapes=[
            vmem(3, *strips),
            pltpu.VMEM(mask.shape, jnp.int32),
            vmem(*scale.shape),
            vmem(3, order, *lines, *tile),
            vmem(3, order, *lines, *tile),
            vmem(3, *strips[1:]),
            vmem(2, *strips[1:]),
            vmem(2, 2, *tile),
            vmem(2, *lines, *tile),
            vmem(3, *lines, *tile),
            vmem(3, *lines, *tile),
            vmem(3, *lines, *tile),
            vmem(2, *tile),
            vmem(2, *tile),
            vmem(2, 3, *lines, *tile),
            vmem(3, 2, 2, *lines, *tile),
            vmem(order, *lines, *tile),
            vmem(triples, *tile),
            vmem(*lines, *tile),
            vmem(2, *lines, *tile),
            vmem(2, *lines, *tile),
            vmem(2, *tile),
            vmem(2, *tile),
            vmem(len(corners), *tile),
            vmem(len(corners), *tile),
        ]
        + [sems(shape) for shape in pairs],
        compiler_params=pltpu.CompilerParams(
            collective_id=0, has_side_effects=True, vmem_limit_bytes=32 << 20
        ),
    )(*[pltpu.with_memory_space_constraint(z, pltpu.HBM) for z in (velocity, mask, scale)])
    return pl.pallas_call(
        functools.partial(deliver, brick),
        out_shape=(
            jax.ShapeDtypeStruct(velocity.shape[1:], f32),
            jax.ShapeDtypeStruct(mask.shape, f32),
        ),
        in_specs=[whole] * 2,
        out_specs=(remote, remote),
        scratch_shapes=[sems((1 + ex * order,))],
        compiler_params=pltpu.CompilerParams(vmem_limit_bytes=16 << 20),
    )(packed, part)


def solution(mesh):
    counts = tuple(mesh.shape[name] for name in names)
    return jax.shard_map(
        functools.partial(shards, counts),
        mesh=mesh,
        in_specs=(P(None, "gx", "gy", "gz"), P("gx", "gy", "gz"), P("gx", "gy", "gz")),
        out_specs=(P("gx", "gy", "gz"), P("gx", "gy", "gz")),
        check_vma=False,
    )
```
